128 devices in a mesh: lat: 16 (over y, z), lon: 8 (over x, core).
Axes of the slice: x: 4, y: 4, z: 4, core: 2. Of those that a mesh axis runs over, the one named last changes fastest.
Arguments:
- fields: bfloat16 [1, 1024, 512, 384], P(None, 'lat', 'lon'), may hold values from -6 to 6
- land: int32 [1024, 512], P('lat', 'lon'), may hold values from 0 to 1
- norm_gains: float32 [4, 384], replicated, may hold values from 0.1 to 1.9
- qkv_weight: bfloat16 [2, 384, 1152], replicated, may hold values from -9 to 9
- rel_bias: float32 [2, 12, 225], replicated, may hold values from -4 to 4
- proj_weight: bfloat16 [2, 384, 384], replicated, may hold values from -0.3125 to 0.3125
- up_weight: bfloat16 [2, 384, 1536], replicated, may hold values from -0.3125 to 0.3125
- down_weight: bfloat16 [2, 1536, 384], replicated, may hold values from -0.15625 to 0.15625
Outputs:
- evolved: bfloat16 [1, 1024, 512, 384], P(None, 'lat', 'lon')
The draws below stay inside these ranges and needn't reach their ends.
All inputs are finite; a program needn't handle non-finite values.
Results may differ from the reference program's by a relative error of at most 0.013.
Values may be sent and summed in bfloat16 or wider, within the bound.
No kernel may reach another device: no remote copies, remote signals or barrier semaphores. Data moves between devices by JAX's collectives and lax.ppermute only.
A program may use at most 256 MiB of HBM per device.

```python
import jax
import jax.numpy as jnp
import numpy as np
from jax import lax

C = 384
HEADS = 12
HID = 1536
WIN = 8
SHIFT = 4
MEMB = 1
LAT = 1024
LON = 512


def draw_qkv_weight(key, part):
    entries = jnp.clip(jax.random.normal(key, (2, C, 3 * C), jnp.float32), -6.0, 6.0) / jnp.sqrt(jnp.float32(C))
    return entries.astype(jnp.bfloat16)


def draw_land(key, part):
    block_rows = LAT // WIN
    block_cols = LON // WIN
    count = 8
    key_top, key_left, key_high, key_wide, key_coast, key_bits = jax.random.split(jax.random.fold_in(key, 71), 6)
    tops = jax.random.randint(key_top, (count,), 0, block_rows)
    lefts = jax.random.randint(key_left, (count,), 0, block_cols)
    highs = jax.random.randint(key_high, (count,), 1, block_rows // 3 + 2)
    wides = jax.random.randint(key_wide, (count,), 1, block_cols // 4 + 2)
    row_at = lax.broadcasted_iota(jnp.int32, (count, block_rows, block_cols), 1)
    col_at = lax.broadcasted_iota(jnp.int32, (count, block_rows, block_cols), 2)
    inside = (row_at >= tops[:, None, None]) & (row_at < (tops + highs)[:, None, None])
    inside = inside & (col_at >= lefts[:, None, None]) & (col_at < (lefts + wides)[:, None, None])
    window_land = jnp.any(inside, axis=0)
    coast = jax.random.randint(key_coast, (block_rows, block_cols), 0, 4) == 0
    token_land = jnp.repeat(jnp.repeat(window_land, WIN, axis=0), WIN, axis=1)
    token_coast = jnp.repeat(jnp.repeat(coast, WIN, axis=0), WIN, axis=1)
    coin = jax.random.randint(key_bits, (LAT, LON), 0, 2) == 1
    return (token_land & ~(token_coast & coin)).astype(jnp.int32)


def levels(stream_key, shape, cuts, low, top_value):
    def one(axis_at, parts):
        heights = jax.random.uniform(jax.random.fold_in(jax.random.fold_in(stream_key, 6), axis_at), (parts,), jnp.float32, low / len(cuts), top_value / len(cuts))
        return jnp.repeat(jnp.exp(heights), shape[axis_at] // parts).reshape((-1,) + (1,) * (len(shape) - axis_at - 1))

    level = one(*cuts[0])
    for cut in cuts[1:]:
        level = level * one(*cut)
    return level


def centred(key, shape, scale, reach, pieces=(), kind=jnp.bfloat16):
    values = jax.random.normal(key, shape, jnp.float32) * scale
    if len(pieces) > 0:
        values = levels(key, shape, pieces, -0.22, 0.18) * values
    return jnp.clip(values, min=-reach, max=reach).astype(kind)


def setup_inputs(seed: int = 0) -> dict:
    seeds = jax.random.split(jax.random.key(seed), 9)
    return {
        "fields": centred(seeds[0], (MEMB, LAT, LON, C), 1.0, 6.0, ((1, 16), (2, 8))),
        "land": draw_land(jax.random.fold_in(seeds[8], 71), 0),
        "norm_gains": jnp.clip(1.0 + 0.18 * jax.random.normal(seeds[2], (4, C), jnp.float32), 0.1, 1.9),
        "qkv_weight": draw_qkv_weight(jax.random.fold_in(seeds[8], 71), 0),
        "rel_bias": centred(seeds[4], (2, HEADS, (2 * WIN - 1) * (2 * WIN - 1)), 1.0, 4.0, (), jnp.float32),
        "proj_weight": centred(seeds[5], (2, C, C), C ** -0.5, 0.3125),
        "up_weight": centred(seeds[6], (2, C, HID), C ** -0.5, 0.3125),
        "down_weight": centred(seeds[7], (2, HID, C), HID ** -0.5, 0.15625),
    }


EPS = 1e-05

def bias_index():
    places = np.arange(WIN * WIN)
    row_pos = places // WIN
    col_pos = places % WIN
    return (row_pos[:, None] - row_pos[None, :] + WIN - 1) * (2 * WIN - 1) + (col_pos[:, None] - col_pos[None, :] + WIN - 1)

def layer_norm(values, gain):
    floats = values.astype(jnp.float32)
    center = lax.optimization_barrier(jnp.mean(floats, axis=-1, keepdims=True))
    spread = lax.optimization_barrier(jnp.mean(jnp.square(floats - center), axis=-1, keepdims=True))
    return ((floats - center) * lax.rsqrt(spread + EPS) * gain).astype(jnp.bfloat16)

def to_windows(grid):
    members, grid_rows, grid_cols, features = grid.shape
    tiles = grid.reshape(members, grid_rows // WIN, WIN, grid_cols // WIN, WIN, features)
    return tiles.transpose(0, 1, 3, 2, 4, 5).reshape(-1, WIN * WIN, features)

def from_windows(tiles, members, grid_rows, grid_cols):
    features = tiles.shape[-1]
    grid = tiles.reshape(members, grid_rows // WIN, grid_cols // WIN, WIN, WIN, features)
    return grid.transpose(0, 1, 3, 2, 4, 5).reshape(members, grid_rows, grid_cols, features)

def window_attention(packed, ocean_tiles, bias_table):
    count = packed.shape[0]
    width_all = packed.shape[-1] // 3
    head_size = width_all // HEADS
    queries = packed[..., :width_all].reshape(count, WIN * WIN, HEADS, head_size).astype(jnp.float32)
    keys_part = packed[..., width_all:2 * width_all].reshape(count, WIN * WIN, HEADS, head_size).astype(jnp.float32)
    values = packed[..., 2 * width_all:].reshape(count, WIN * WIN, HEADS, head_size).astype(jnp.float32)
    bias = bias_table[:, bias_index()]
    scores = jnp.einsum('nqhd,nkhd->nhqk', queries, keys_part) / jnp.sqrt(jnp.float32(head_size)) + bias[None]
    allowed = (ocean_tiles[:, None, None, :] == 1) | jnp.eye(WIN * WIN, dtype=bool)[None, None]
    scores = jnp.where(allowed, scores, -jnp.inf)
    top = lax.optimization_barrier(jnp.max(scores, axis=-1, keepdims=True))
    weights = jnp.exp(scores - top)
    weights = (weights / lax.optimization_barrier(jnp.sum(weights, axis=-1, keepdims=True))).astype(jnp.bfloat16)
    mixed = jnp.einsum('nhqk,nkhd->nqhd', weights.astype(jnp.float32), values)
    return mixed.reshape(count, WIN * WIN, width_all).astype(jnp.bfloat16)

def grid_attention(packed_grid, ocean_grid, bias_table):
    members, grid_rows, grid_cols, depth = packed_grid.shape
    bands = grid_rows // WIN
    stacked = packed_grid.reshape(members, bands, WIN, grid_cols, depth).transpose(1, 0, 2, 3, 4)
    ocean_stack = ocean_grid.reshape(members, bands, WIN, grid_cols).transpose(1, 0, 2, 3)

    def one_band(pair):
        band_qkv, band_ocean = pair
        tiles = to_windows(band_qkv)
        ocean_tiles = to_windows(band_ocean[..., None])[..., 0]
        mixed = window_attention(tiles, ocean_tiles, bias_table)
        return from_windows(mixed, members, WIN, grid_cols)
    result = lax.map(one_band, (stacked, ocean_stack))
    return result.transpose(1, 0, 2, 3, 4).reshape(members, grid_rows, grid_cols, -1)

def project_qkv(grid, gain, weight):
    features = grid.shape[-1]
    normed = layer_norm(grid, gain).reshape(-1, features)
    packed = jnp.dot(normed, weight, preferred_element_type=jnp.float32).astype(jnp.bfloat16)
    return packed.reshape(grid.shape[:-1] + (weight.shape[1],))

def finish_block(fields, attended, proj_w, gain_two, up_w, down_w):
    features = fields.shape[-1]
    flat = fields.reshape(-1, features)
    mixed = attended.reshape(-1, features)
    mid_state = (flat.astype(jnp.float32) + jnp.dot(mixed, proj_w, preferred_element_type=jnp.float32)).astype(jnp.bfloat16)
    mid_state = lax.optimization_barrier(mid_state)
    normed_two = layer_norm(mid_state, gain_two)
    expanded = jax.nn.gelu(jnp.dot(normed_two, up_w, preferred_element_type=jnp.float32), approximate=True).astype(jnp.bfloat16)
    result = mid_state.astype(jnp.float32) + jnp.dot(expanded, down_w, preferred_element_type=jnp.float32)
    return result.astype(jnp.bfloat16).reshape(fields.shape)

def reference(fields, land, norm_gains, qkv_weight, rel_bias, proj_weight, up_weight, down_weight):
    members = fields.shape[0]
    ocean = jnp.broadcast_to((1 - land).astype(jnp.int32)[None], (members,) + land.shape)
    first_qkv = project_qkv(fields, norm_gains[0], qkv_weight[0])
    first_mix = grid_attention(first_qkv, ocean, rel_bias[0])
    settled = finish_block(fields, first_mix, proj_weight[0], norm_gains[1], up_weight[0], down_weight[0])
    wide_fields = jnp.concatenate([settled[:, :, -SHIFT:], settled, settled[:, :, :SHIFT]], axis=2)
    wide_fields = jnp.pad(wide_fields, ((0, 0), (SHIFT, SHIFT), (0, 0), (0, 0)))
    wide_ocean = jnp.concatenate([ocean[:, :, -SHIFT:], ocean, ocean[:, :, :SHIFT]], axis=2)
    wide_ocean = jnp.pad(wide_ocean, ((0, 0), (SHIFT, SHIFT), (0, 0)))
    wide_qkv = project_qkv(wide_fields, norm_gains[2], qkv_weight[1])
    shifted = grid_attention(wide_qkv, wide_ocean, rel_bias[1])[:, SHIFT:-SHIFT, SHIFT:-SHIFT]
    return finish_block(settled, shifted, proj_weight[1], norm_gains[3], up_weight[1], down_weight[1])
```

```python
import functools

import jax
import jax.numpy as jnp
import numpy as np
from jax import lax
from jax.experimental import pallas as pl
from jax.experimental.pallas import tpu as pltpu
from jax.sharding import PartitionSpec as P

HEADS = 12
WIN = 8
SHIFT = 4
EPS = 1e-05
C = 384
HID = 1536
TOK = WIN * WIN
BIG = 1e30
LOG2E = 1.4426950408889634
QSCALE = LOG2E / (C // HEADS) ** 0.5
BF = jnp.bfloat16
F32 = jnp.float32


def places(shifted):
    slot = np.arange(TOK)
    col = slot % WIN
    return slot // WIN, (col + SHIFT) % WIN if shifted else col


def bias_selector(shifted):
    row, col = places(shifted)
    index = (row[None, :] - row[:, None] + WIN - 1) * (2 * WIN - 1) + (col[None, :] - col[:, None] + WIN - 1)
    index = np.concatenate([index, index], axis=1).reshape(-1)
    table = np.zeros(((2 * WIN - 1) ** 2, index.size), np.float32)
    table[index, np.arange(index.size)] = 1.0
    return table


def bias_tiles(table, shifted):
    table = table * LOG2E
    high = table.astype(BF)
    low = (table - high.astype(F32)).astype(BF)
    both = jnp.concatenate([high, low], axis=0)
    picked = jnp.dot(both, jnp.asarray(bias_selector(shifted), BF), preferred_element_type=F32)
    return (picked[:HEADS] + picked[HEADS:]).reshape(HEADS, TOK, 2 * TOK)


def flag_matrices(windows, tiles, shifted):
    slot = np.arange(TOK) % WIN
    lane = np.arange(128)
    match = (lane[None, :] % WIN == slot[:, None]) & (lane[None, :] < tiles * WIN)
    win = np.repeat(np.arange(windows), TOK)
    if not shifted:
        return match.astype(np.float32), (lane[:, None] // WIN == win[None, :]).astype(np.float32)
    low = match & (slot[:, None] < SHIFT)
    high = match & (slot[:, None] >= SHIFT)
    spread = np.concatenate([low, high], axis=1).astype(np.float32)
    pick_low = lane[:, None] // WIN == win[None, :] % tiles
    pick_high = lane[:, None] // WIN == (win[None, :] - 1) % tiles
    return spread, np.concatenate([pick_low, pick_high], axis=0).astype(np.float32)


def normed(values, gain):
    center = jnp.mean(values, axis=-1, keepdims=True)
    moved = values - center
    spread = jnp.mean(moved * moved, axis=-1, keepdims=True)
    return (moved * lax.rsqrt(spread + EPS) * gain).astype(BF)


def dot_nt(a, b):
    return lax.dot_general(a, b, (((1,), (1,)), ((), ())), preferred_element_type=F32)


def dot_nn(a, b):
    return jnp.dot(a, b, preferred_element_type=F32)


def attend_pair(q_ref, k_ref, vt_ref, bias_ref, mask, first, second):
    lane_head = lax.broadcasted_iota(jnp.int32, (TOK, 128), 1) // 32
    lane = lax.broadcasted_iota(jnp.int32, (TOK, 2 * TOK), 1)
    zero = jnp.zeros((TOK, 128), BF)
    rows = (pl.ds(first * TOK, TOK), pl.ds(second * TOK, TOK))
    if second == first + 1 and first % 2 == 0:
        values = vt_ref[:, pl.ds(first * TOK, 2 * TOK)]
    else:
        values = vt_ref[:, pl.ds(first * TOK, 2 * TOK)]
        values = jnp.concatenate([values[:, :TOK], values[:, :TOK]], axis=1)
    outs = []
    for group in range(3):
        lanes = pl.ds(group * 128, 128)
        keys = jnp.concatenate([k_ref[rows[0], lanes], k_ref[rows[1], lanes]], axis=1)
        q0, q1 = q_ref[rows[0], lanes], q_ref[rows[1], lanes]
        for half in range(2):
            blocks = []
            for head in (2 * half, 2 * half + 1):
                here = lane_head == head
                blocks.append(jnp.concatenate([jnp.where(here, q0, zero), zero], axis=1))
                blocks.append(jnp.concatenate([zero, jnp.where(here, q1, zero)], axis=1))
            scores = dot_nt(keys, jnp.concatenate(blocks, axis=0))
            for j in range(2):
                head = group * 4 + 2 * half + j
                s = scores[:, j * 128 : (j + 1) * 128] + bias_ref[head] + mask
                top = jnp.max(s, axis=0, keepdims=True)
                e = jnp.exp2(s - top)
                total = jnp.sum(e, axis=0, keepdims=True)
                p = (e * (1.0 / total)).astype(BF)
                spread = jnp.concatenate(
                    [jnp.where(lane < TOK, p, jnp.zeros_like(p)), jnp.where(lane < TOK, jnp.zeros_like(p), p)], axis=0
                )
                outs.append(dot_nn(values[head * 32 : (head + 1) * 32], spread))
    return jnp.concatenate(outs, axis=0)


def pair_mask(flags, spread_ref, pick_ref):
    rows = jnp.broadcast_to(flags.astype(F32)[:, None, :], (WIN, WIN, 128)).reshape(TOK, 128)
    if spread_ref.shape[1] == 256:
        rows = jnp.concatenate([rows, rows], axis=1)
    return dot_nn((rows * spread_ref[...]).astype(BF), pick_ref[...]) * -BIG


def finish(x, mixed, proj_ref, gain, up_ref, down_ref):
    mid = (x + dot_nn(mixed, proj_ref[...])).astype(BF).astype(F32)
    hidden = dot_nn(normed(mid, gain), up_ref[...])
    hidden = jax.nn.gelu(hidden, approximate=True).astype(BF)
    return mid + dot_nn(hidden, down_ref[...])


def project(x_win, gain, qkv_ref, wvt_ref, q_ref, k_ref, vt_ref):
    packed = normed(x_win, gain)
    q_ref[...] = (dot_nn(packed, qkv_ref[:, :C]) * QSCALE).astype(BF)
    k_ref[...] = dot_nn(packed, qkv_ref[:, C : 2 * C]).astype(BF)
    vt_ref[...] = dot_nt(wvt_ref[...], packed).astype(BF)


def first_kernel(x_ref, land_ref, gain_ref, qkv_ref, wvt_ref, bias_ref, spread_ref, pick_ref, proj_ref, up_ref, down_ref,
                 out_ref, xw_ref, q_ref, k_ref, vt_ref, o_ref):
    windows = 8
    for r in range(WIN):
        for w in range(windows):
            xw_ref[pl.ds(w * TOK + r * WIN, WIN), :] = x_ref[r, pl.ds(w * WIN, WIN), :].astype(F32)
    project(xw_ref[...], gain_ref[0:1], qkv_ref, wvt_ref, q_ref, k_ref, vt_ref)
    neg = pair_mask(land_ref[...], spread_ref, pick_ref)
    key = lax.broadcasted_iota(jnp.int32, (TOK, 128), 0)
    own = lax.broadcasted_iota(jnp.int32, (TOK, 128), 1) % TOK == key
    for pair in range(windows // 2):
        mask = jnp.where(own, 0.0, neg[:, pair * 128 : (pair + 1) * 128])
        o_ref[pl.ds(pair * 128, 128), :] = attend_pair(q_ref, k_ref, vt_ref, bias_ref, mask, 2 * pair, 2 * pair + 1).astype(BF).T
    result = finish(xw_ref[...], o_ref[...], proj_ref, gain_ref[1:2], up_ref, down_ref)
    for r in range(WIN):
        for w in range(windows):
            out_ref[r, pl.ds(w * WIN, WIN), :] = result[w * TOK + r * WIN : w * TOK + (r + 1) * WIN].astype(BF)


def second_kernel(x_ref, own_ref, land_ref, gain_ref, qkv_ref, wvt_ref, bias_ref, spread_ref, pick_ref, proj_ref, up_ref, down_ref,
                  out_ref, xw_ref, q_ref, k_ref, vt_ref, o_ref, att_ref):
    windows = 9
    step = pl.program_id(0)
    low = lax.broadcasted_iota(jnp.int32, (WIN, C), 0) < SHIFT
    for r in range(WIN):
        tiles = [x_ref[r, pl.ds(t * WIN, WIN), :].astype(F32) for t in range(windows)]
        for w in range(windows):
            xw_ref[pl.ds(w * TOK + r * WIN, WIN), :] = jnp.where(low, tiles[w], tiles[(w - 1) % windows])
    xw_ref[pl.ds(windows * TOK, TOK), :] = jnp.zeros((TOK, C), F32)
    project(xw_ref[...], gain_ref[0:1], qkv_ref, wvt_ref, q_ref, k_ref, vt_ref)
    neg = pair_mask(land_ref[...], spread_ref, pick_ref)
    key = lax.broadcasted_iota(jnp.int32, (TOK, 128), 0)
    own = lax.broadcasted_iota(jnp.int32, (TOK, 128), 1) % TOK == key
    for pair in range(5):
        mask = jnp.where(own, 0.0, neg[:, pair * 128 : (pair + 1) * 128])
        o_ref[pl.ds(pair * 128, 128), :] = attend_pair(q_ref, k_ref, vt_ref, bias_ref, mask, 2 * pair, 2 * pair + 1).T
    for t in range(8):
        for r in range(WIN):
            left = o_ref[pl.ds(t * TOK + r * WIN, WIN), :]
            right = o_ref[pl.ds((t + 1) * TOK + r * WIN, WIN), :]
            att_ref[r + SHIFT, pl.ds(t * WIN, WIN), :] = jnp.where(low, left, right)

    @pl.when(step > 0)
    def _():
        mixed = att_ref[0:WIN].reshape(WIN * 64, C).astype(BF)
        x = own_ref[...].astype(F32).reshape(WIN * 64, C)
        result = finish(x, mixed, proj_ref, gain_ref[1:2], up_ref, down_ref)
        out_ref[...] = result.reshape(WIN, 64, C).astype(BF)

    att_ref[0:SHIFT] = att_ref[WIN : WIN + SHIFT]


def whole(shape):
    return pl.BlockSpec(shape, lambda i: (0,) * len(shape), pipeline_mode=pl.Buffered(1))


def layer_weights(layer, norm_gains, qkv_weight, proj_weight, up_weight, down_weight):
    qkv = qkv_weight[layer]
    return (norm_gains[2 * layer : 2 * layer + 2], qkv, qkv[:, 2 * C :].T, proj_weight[layer], up_weight[layer], down_weight[layer])


def weight_specs():
    return [whole((2, C)), whole((C, 3 * C)), whole((C, C)), whole((HEADS, TOK, 128))]


def first_layer(x, land, gains, qkv, wvt, proj, up, down, bias):
    rows, cols, _ = x.shape
    windows = cols // WIN
    tokens = windows * TOK
    spread, pick = flag_matrices(windows, windows, False)
    land = jnp.pad(land, ((0, 0), (0, 128 - cols)))
    return pl.pallas_call(
        first_kernel,
        grid=(rows // WIN,),
        in_specs=[
            pl.BlockSpec((WIN, cols, C), lambda i: (i, 0, 0)),
            pl.BlockSpec((WIN, 128), lambda i: (i, 0)),
            *weight_specs(),
            whole(spread.shape),
            whole(pick.shape),
            whole((C, C)),
            whole((C, HID)),
            whole((HID, C)),
        ],
        out_specs=pl.BlockSpec((WIN, cols, C), lambda i: (i, 0, 0)),
        out_shape=jax.ShapeDtypeStruct((rows, cols, C), BF),
        scratch_shapes=[
            pltpu.VMEM((tokens, C), F32),
            pltpu.VMEM((tokens, C), BF),
            pltpu.VMEM((tokens, C), BF),
            pltpu.VMEM((C, tokens), BF),
            pltpu.VMEM((tokens, C), BF),
        ],
        compiler_params=pltpu.CompilerParams(vmem_limit_bytes=56 << 20),
        name="first_layer",
    )(x, land, gains, qkv, wvt, bias, jnp.asarray(spread), jnp.asarray(pick, BF), proj, up, down)


def second_layer(wide, own, land, gains, qkv, wvt, proj, up, down, bias):
    rows, cols, _ = wide.shape
    windows = cols // WIN
    tokens = (windows + 1) * TOK
    spread, pick = flag_matrices(windows + 1, windows, True)
    land = jnp.pad(land, ((0, 0), (0, 128 - cols)))
    return pl.pallas_call(
        second_kernel,
        grid=(rows // WIN,),
        in_specs=[
            pl.BlockSpec((WIN, cols, C), lambda i: (i, 0, 0)),
            pl.BlockSpec((WIN, 64, C), lambda i: (jnp.maximum(i - 1, 0), 0, 0)),
            pl.BlockSpec((WIN, 128), lambda i: (i, 0)),
            *weight_specs(),
            whole(spread.shape),
            whole(pick.shape),
            whole((C, C)),
            whole((C, HID)),
            whole((HID, C)),
        ],
        out_specs=pl.BlockSpec((WIN, 64, C), lambda i: (jnp.maximum(i - 1, 0), 0, 0)),
        out_shape=jax.ShapeDtypeStruct(own.shape, BF),
        scratch_shapes=[
            pltpu.VMEM((tokens, C), F32),
            pltpu.VMEM((tokens, C), BF),
            pltpu.VMEM((tokens, C), BF),
            pltpu.VMEM((C, tokens), BF),
            pltpu.VMEM((tokens, C), F32),
            pltpu.VMEM((WIN + SHIFT, 64, C), F32),
        ],
        compiler_params=pltpu.CompilerParams(vmem_limit_bytes=56 << 20),
        name="second_layer",
    )(wide, own, land, gains, qkv, wvt, bias, jnp.asarray(spread), jnp.asarray(pick, BF), proj, up, down)


def ring(axis, periodic):
    count = lax.axis_size(axis)
    forward = [(i, i + 1) for i in range(count - 1)]
    if periodic:
        forward.append((count - 1, 0))
    return forward, [(b, a) for a, b in forward]


def widen(block):
    forward, backward = ring("lon", True)
    left = lax.ppermute(block[:, -SHIFT:], "lon", forward)
    right = lax.ppermute(block[:, :SHIFT], "lon", backward)
    block = jnp.concatenate([block, right, left], axis=1)
    forward, backward = ring("lat", False)
    above = lax.ppermute(block[-SHIFT:], "lat", forward)
    below = lax.ppermute(block[:SHIFT], "lat", backward)
    return jnp.concatenate([above, block, below], axis=0)


def shards(fields, land, norm_gains, qkv_weight, rel_bias, proj_weight, up_weight, down_weight):
    rest = (norm_gains, qkv_weight, proj_weight, up_weight, down_weight)
    wide_land = 1 - widen(1 - land)
    settled = first_layer(fields[0], land, *layer_weights(0, *rest), bias_tiles(rel_bias[0], False))
    evolved = second_layer(widen(settled), settled, wide_land, *layer_weights(1, *rest), bias_tiles(rel_bias[1], True))
    return evolved[None]


def solution(mesh):
    return jax.shard_map(
        shards,
        mesh=mesh,
        in_specs=(P(None, "lat", "lon", None), P("lat", "lon"), P(), P(), P(), P(), P(), P()),
        out_specs=P(None, "lat", "lon", None),
        check_vma=False,
    )
```

```python
import functools

import jax
import jax.numpy as jnp
import numpy as np
from jax import lax
from jax.experimental import pallas as pl
from jax.experimental.pallas import tpu as pltpu
from jax.sharding import PartitionSpec as P

HEADS = 12
WIN = 8
SHIFT = 4
EPS = 1e-05
C = 384
HID = 1536
TOK = WIN * WIN
BIG = 1e30
LOG2E = 1.4426950408889634
QSCALE = LOG2E / (C // HEADS) ** 0.5
BF = jnp.bfloat16
F32 = jnp.float32


WIDE = C + 128
SPAN = 2 * WIN - 1


def bias_selector(shifted):
    slot = np.arange(WIN)
    col = (slot + SHIFT) % WIN if shifted else slot
    table = np.zeros((256, WIN, 128), np.float32)
    for key in range(WIN):
        for far in range(SPAN):
            for query in range(WIN):
                table[far * SPAN + col[query] - col[key] + WIN - 1, key, far * WIN + query] = 1.0
    return table.reshape(256, WIN * 128)


def flag_matrices(windows):
    slot = np.arange(TOK) % WIN
    lane = np.arange(windows * WIN)
    spread = lane[None, :] % WIN == slot[:, None]
    pick = lane[:, None] // WIN == np.repeat(np.arange(windows), 128)[None, :]
    return spread.astype(np.float32), pick.astype(np.float32)


def normed(values, gain):
    center = jnp.mean(values, axis=-1, keepdims=True)
    moved = values - center
    spread = jnp.mean(moved * moved, axis=-1, keepdims=True)
    return (moved * lax.rsqrt(spread + EPS) * gain).astype(BF)


def dot_nt(a, b):
    return lax.dot_general(a, b, (((1,), (1,)), ((), ())), preferred_element_type=F32)


def dot_nn(a, b):
    return jnp.dot(a, b, preferred_element_type=F32)


def score_pair(qt_ref, k_ref, bias_ref, s_ref, mask, pair):
    here = pl.ds(pair * 128, 128)
    first = lax.broadcasted_iota(jnp.int32, (TOK, 128), 1) < TOK
    zero = jnp.zeros((32, 128), BF)
    for group in range(3):
        keys = k_ref[here, pl.ds(group * 128, 128)]
        for half in range(2):
            base = group * 4 + 2 * half
            columns = []
            for j in range(2):
                blocks = [zero] * 4
                blocks[2 * half + j] = qt_ref[pl.ds((base + j) * 32, 32), here]
                columns.append(jnp.concatenate(blocks, axis=0))
            scores = dot_nn(keys, jnp.concatenate(columns, axis=1))
            for j in range(2):
                both = scores[:, j * 128 : (j + 1) * 128]
                s_ref[pair % 2, base + j] = jnp.where(first, both[:TOK], both[TOK:]) + (bias_ref[base + j] + mask)


def weigh_pair(s_ref, p_ref, pair):
    side = lax.broadcasted_iota(jnp.int32, (1, 128), 1) < TOK
    for head in range(HEADS):
        s = s_ref[pair % 2, head]
        e = jnp.exp2(s - jnp.max(s, axis=0, keepdims=True))
        inv = 1.0 / jnp.sum(e, axis=0, keepdims=True)
        lanes = pl.ds(head % 2 * 128, 128)
        p_ref[pair % 2, head // 2, :TOK, lanes] = (e * jnp.where(side, inv, 0.0)).astype(BF)
        p_ref[pair % 2, head // 2, TOK:, lanes] = (e * jnp.where(side, 0.0, inv)).astype(BF)


def mix_pair(vt_ref, p_ref, ot_ref, pair):
    here = pl.ds(pair * 128, 128)
    for two in range(HEADS // 2):
        mixed = dot_nn(vt_ref[pl.ds(two * 64, 64), here], p_ref[pair % 2, two])
        ot_ref[pl.ds(two * 64, 32), here] = mixed[:32, :128]
        ot_ref[pl.ds(two * 64 + 32, 32), here] = mixed[32:, 128:]


def attend(qt_ref, k_ref, vt_ref, bias_ref, s_ref, p_ref, ot_ref, ocean, pairs):
    key = lax.broadcasted_iota(jnp.int32, (TOK, 128), 0)
    lane = lax.broadcasted_iota(jnp.int32, (TOK, 128), 1)

    def score(pair):
        flags = jnp.where(lane < TOK, ocean(2 * pair), ocean(2 * pair + 1))
        mask = jnp.where((lane % TOK == key) | (flags > 0.5), 0.0, -BIG)
        score_pair(qt_ref, k_ref, bias_ref, s_ref, mask, pair)

    score(0)
    for pair in range(pairs):
        if pair + 1 < pairs:
            score(pair + 1)
        weigh_pair(s_ref, p_ref, pair)
        mix_pair(vt_ref, p_ref, ot_ref, pair)


def finish(x, mixed, proj_ref, gain, up_ref, down_ref):
    mid = (x + dot_nn(mixed, proj_ref[...])).astype(BF).astype(F32)
    hidden = dot_nn(normed(mid, gain), up_ref[...])
    hidden = jax.nn.gelu(hidden, approximate=True).astype(BF)
    return mid + dot_nn(hidden, down_ref[...])


def project(x_win, gain, qkv_ref, wt_ref, qt_ref, k_ref, vt_ref):
    packed = normed(x_win, gain)
    qt_ref[...] = (dot_nt(wt_ref[:C], packed) * QSCALE).astype(BF)
    k_ref[...] = dot_nn(packed, qkv_ref[:, C : 2 * C]).astype(BF)
    vt_ref[...] = dot_nt(wt_ref[C:], packed).astype(BF)


def prepare(qkv_ref, table_ref, select_ref, wt_ref, tab_ref, row_ref, bias_ref):
    @pl.when(pl.program_id(0) == 0)
    def _():
        wt_ref[:C] = qkv_ref[:, :C].T
        wt_ref[C:] = qkv_ref[:, 2 * C :].T
        tab_ref[...] = jnp.zeros_like(tab_ref)
        tab_ref[:HEADS, : SPAN * SPAN] = table_ref[...] * LOG2E
        high = tab_ref[...].astype(BF)
        low = (tab_ref[...] - high.astype(F32)).astype(BF)
        picked = dot_nn(high, select_ref[...]) + dot_nn(low, select_ref[...])
        for key in range(WIN):
            for head in range(HEADS):
                row_ref[head, key : key + 1] = picked[head : head + 1, key * 128 : (key + 1) * 128]
        first = lax.broadcasted_iota(jnp.int32, (WIN, 128), 1) < TOK
        for head in range(HEADS):
            rows = row_ref[head]
            for row in range(WIN):
                back = (WIN - 1 - row) * WIN
                left = pltpu.roll(rows, (128 - back) % 128, 1)
                right = pltpu.roll(rows, (TOK - back) % 128, 1)
                bias_ref[head, row * WIN : (row + 1) * WIN] = jnp.where(first, left, right)


def first_kernel(x_ref, land_ref, gain_ref, qkv_ref, table_ref, select_ref, proj_ref, up_ref, down_ref, spread_ref, pick_ref,
                 out_ref, wt_ref, tab_ref, row_ref, bias_ref, xw_ref, qt_ref, k_ref, vt_ref, s_ref, p_ref, ot_ref, o_ref):
    windows = 8
    prepare(qkv_ref, table_ref, select_ref, wt_ref, tab_ref, row_ref, bias_ref)
    for r in range(WIN):
        for w in range(windows):
            xw_ref[pl.ds(w * TOK + r * WIN, WIN), :] = x_ref[0, r, pl.ds(w * WIN, WIN), :].astype(F32)
    project(xw_ref[...], gain_ref[0:1], qkv_ref, wt_ref, qt_ref, k_ref, vt_ref)
    flags = (1 - land_ref[...]).astype(F32)
    rows = jnp.broadcast_to(flags[:, None, :], (WIN, WIN, windows * WIN)).reshape(TOK, windows * WIN)
    ocean = dot_nn((rows * spread_ref[...]).astype(BF), pick_ref[...])
    attend(qt_ref, k_ref, vt_ref, bias_ref, s_ref, p_ref, ot_ref, lambda w: ocean[:, w * 128 : (w + 1) * 128], windows // 2)
    o_ref[...] = ot_ref[...].astype(BF).T
    result = finish(xw_ref[...], o_ref[...], proj_ref, gain_ref[1:2], up_ref, down_ref)
    for r in range(WIN):
        for w in range(windows):
            out_ref[r, pl.ds(w * WIN, WIN), :C] = result[w * TOK + r * WIN : w * TOK + (r + 1) * WIN].astype(BF)
            out_ref[r, pl.ds(w * WIN, WIN), C:] = ocean[r * WIN : (r + 1) * WIN, w * 128 : (w + 1) * 128].astype(BF)


def second_kernel(low_ref, high_ref, low_side_ref, high_side_ref, above_ref, below_ref, own_ref,
                  gain_ref, qkv_ref, table_ref, select_ref, proj_ref, up_ref, down_ref,
                  out_ref, wt_ref, tab_ref, row_ref, bias_ref, xw_ref, qt_ref, k_ref, vt_ref, s_ref, p_ref, ot_ref, o_ref, att_ref):
    windows = 9
    step = pl.program_id(0)
    last = step == pl.num_programs(0) - 1
    prepare(qkv_ref, table_ref, select_ref, wt_ref, tab_ref, row_ref, bias_ref)
    low = lax.broadcasted_iota(jnp.int32, (WIN, C), 0) < SHIFT
    low_wide = lax.broadcasted_iota(jnp.int32, (WIN, WIDE), 0) < SHIFT
    for r in range(WIN):
        near, side, far, edge = (low_ref, low_side_ref, above_ref, step == 0) if r < SHIFT else (high_ref, high_side_ref, below_ref, last)
        tiles = []
        for t in range(windows):
            inner = near[r % SHIFT, pl.ds(t * WIN, WIN), :] if t < 8 else side[r % SHIFT]
            tiles.append(jnp.where(edge, far[r % SHIFT, pl.ds(t * WIN, WIN), :].astype(F32), inner.astype(F32)))
        for w in range(windows):
            xw_ref[pl.ds(w * TOK + r * WIN, WIN), :] = jnp.where(low_wide, tiles[w], tiles[(w - 1) % windows])
    xw_ref[pl.ds(windows * TOK, TOK), :] = jnp.zeros((TOK, WIDE), F32)
    project(xw_ref[:, :C], gain_ref[2:3], qkv_ref, wt_ref, qt_ref, k_ref, vt_ref)
    attend(qt_ref, k_ref, vt_ref, bias_ref, s_ref, p_ref, ot_ref, lambda w: xw_ref[pl.ds(w * TOK, TOK), C:], 5)
    o_ref[...] = ot_ref[...].T
    for t in range(8):
        for r in range(WIN):
            left = o_ref[pl.ds(t * TOK + r * WIN, WIN), :]
            right = o_ref[pl.ds((t + 1) * TOK + r * WIN, WIN), :]
            att_ref[r + SHIFT, pl.ds(t * WIN, WIN), :] = jnp.where(low, left, right)

    @pl.when(step > 0)
    def _():
        mixed = att_ref[0:WIN].reshape(WIN * 64, C).astype(BF)
        x = own_ref[...].astype(F32).reshape(WIN * 64, C)
        result = finish(x, mixed, proj_ref, gain_ref[3:4], up_ref, down_ref)
        out_ref[0] = result.reshape(WIN, 64, C).astype(BF)

    att_ref[0:SHIFT] = att_ref[WIN : WIN + SHIFT]


def whole(*shape):
    return pl.BlockSpec(shape, lambda i: (0,) * len(shape), pipeline_mode=pl.Buffered(1))


def of_layer(layer, *shape):
    return pl.BlockSpec((None, *shape), lambda i: (layer, 0, 0), pipeline_mode=pl.Buffered(1))


def weight_specs(layer):
    return [
        whole(4, C),
        of_layer(layer, C, 3 * C),
        of_layer(layer, HEADS, SPAN * SPAN),
        whole(256, WIN * 128),
        of_layer(layer, C, C),
        of_layer(layer, C, HID),
        of_layer(layer, HID, C),
    ]


def scratch(tokens, width):
    return [
        pltpu.VMEM((2 * C, C), BF),
        pltpu.VMEM((16, 256), F32),
        pltpu.VMEM((HEADS, WIN, 128), F32),
        pltpu.VMEM((HEADS, TOK, 128), F32),
        pltpu.VMEM((tokens, width), F32),
        pltpu.VMEM((C, tokens), BF),
        pltpu.VMEM((tokens, C), BF),
        pltpu.VMEM((C, tokens), BF),
        pltpu.VMEM((2, HEADS, TOK, 128), F32),
        pltpu.VMEM((2, HEADS // 2, 128, 256), BF),
        pltpu.VMEM((C, tokens), F32),
    ]


PARAMS = pltpu.CompilerParams(vmem_limit_bytes=56 << 20)


def first_layer(fields, land, weights):
    _, rows, cols, _ = fields.shape
    windows = cols // WIN
    tokens = windows * TOK
    spread, pick = flag_matrices(windows)
    return pl.pallas_call(
        first_kernel,
        grid=(rows // WIN,),
        in_specs=[
            pl.BlockSpec((1, WIN, cols, C), lambda i: (0, i, 0, 0)),
            pl.BlockSpec((WIN, cols), lambda i: (i, 0)),
            *weight_specs(0),
            whole(*spread.shape),
            whole(*pick.shape),
        ],
        out_specs=pl.BlockSpec((WIN, cols, WIDE), lambda i: (i, 0, 0)),
        out_shape=jax.ShapeDtypeStruct((rows, cols, WIDE), BF),
        scratch_shapes=[*scratch(tokens, C), pltpu.VMEM((tokens, C), BF)],
        compiler_params=PARAMS,
        name="first_layer",
    )(fields, land, *weights(False), jnp.asarray(spread), jnp.asarray(pick, BF))


def second_layer(own, side, above, below, weights):
    rows, cols, _ = own.shape
    bands = rows // WIN
    tokens = (cols // WIN + 2) * TOK
    lower = lambda i: (jnp.maximum(2 * i - 1, 0), 0, 0)
    upper = lambda i: (jnp.minimum(2 * i, 2 * bands - 1), 0, 0)
    done = lambda i: jnp.maximum(i - 1, 0)
    return pl.pallas_call(
        second_kernel,
        grid=(bands + 1,),
        in_specs=[
            pl.BlockSpec((SHIFT, cols, WIDE), lower),
            pl.BlockSpec((SHIFT, cols, WIDE), upper),
            pl.BlockSpec((SHIFT, WIN, WIDE), lower),
            pl.BlockSpec((SHIFT, WIN, WIDE), upper),
            whole(SHIFT, cols + WIN, WIDE),
            whole(SHIFT, cols + WIN, WIDE),
            pl.BlockSpec((WIN, cols, C), lambda i: (done(i), 0, 0)),
            *weight_specs(1),
        ],
        out_specs=pl.BlockSpec((1, WIN, cols, C), lambda i: (0, done(i), 0, 0)),
        out_shape=jax.ShapeDtypeStruct((1, rows, cols, C), BF),
        scratch_shapes=[*scratch(tokens, WIDE), pltpu.VMEM((tokens, C), F32), pltpu.VMEM((WIN + SHIFT, cols, C), F32)],
        compiler_params=PARAMS,
        name="second_layer",
    )(own, own, side, side, above, below, own, *weights(True))


def ring(axis, periodic):
    count = lax.axis_size(axis)
    forward = [(i, i + 1) for i in range(count - 1)]
    if periodic:
        forward.append((count - 1, 0))
    return forward, [(b, a) for a, b in forward]


def borders(block):
    forward, backward = ring("lon", True)
    left = lax.ppermute(block[:, -SHIFT:], "lon", forward)
    right = lax.ppermute(block[:, :SHIFT], "lon", backward)
    side = jnp.concatenate([right, left], axis=1)
    forward, backward = ring("lat", False)
    above = lax.ppermute(jnp.concatenate([block[-SHIFT:], side[-SHIFT:]], axis=1), "lat", forward)
    below = lax.ppermute(jnp.concatenate([block[:SHIFT], side[:SHIFT]], axis=1), "lat", backward)
    return side, above, below


def shards(fields, land, norm_gains, qkv_weight, rel_bias, proj_weight, up_weight, down_weight):
    def weights(shifted):
        return (norm_gains, qkv_weight, rel_bias, jnp.asarray(bias_selector(shifted), BF), proj_weight, up_weight, down_weight)

    settled = first_layer(fields, land, weights)
    return second_layer(settled, *borders(settled), weights)


def solution(mesh):
    return jax.shard_map(
        shards,
        mesh=mesh,
        in_specs=(P(None, "lat", "lon", None), P("lat", "lon"), P(), P(), P(), P(), P(), P()),
        out_specs=P(None, "lat", "lon", None),
        check_vma=False,
    )
```

```python
import functools

import jax
import jax.numpy as jnp
import numpy as np
from jax import lax
from jax.experimental import pallas as pl
from jax.experimental.pallas import tpu as pltpu
from jax.sharding import PartitionSpec as P

HEADS = 12
WIN = 8
SHIFT = 4
EPS = 1e-05
C = 384
HID = 1536
TOK = WIN * WIN
BIG = 1e30
LOG2E = 1.4426950408889634
QSCALE = LOG2E / (C // HEADS) ** 0.5
BF = jnp.bfloat16
UP_CHUNK = 256
ORDER_FIRST = "abaabaabababaababaabaab"
ORDER_SECOND = "abaaabaaabaaabaaabaaabab"
F32 = jnp.float32


WIDE = C + 128
SPAN = 2 * WIN - 1


def bias_selector(shifted):
    slot = np.arange(WIN)
    col = (slot + SHIFT) % WIN if shifted else slot
    table = np.zeros((256, WIN, 128), np.float32)
    for key in range(WIN):
        for far in range(SPAN):
            for query in range(WIN):
                table[far * SPAN + col[query] - col[key] + WIN - 1, key, far * WIN + query] = 1.0
    return table.reshape(256, WIN * 128)


def flag_matrices(windows):
    slot = np.arange(TOK) % WIN
    lane = np.arange(windows * WIN)
    spread = lane[None, :] % WIN == slot[:, None]
    pick = lane[:, None] // WIN == np.repeat(np.arange(windows), 128)[None, :]
    return spread.astype(np.float32), pick.astype(np.float32)


def normed(values, gain):
    center = jnp.mean(values, axis=-1, keepdims=True)
    moved = values - center
    spread = jnp.mean(moved * moved, axis=-1, keepdims=True)
    return (moved * lax.rsqrt(spread + EPS) * gain).astype(BF)


def dot_nt(a, b):
    return lax.dot_general(a, b, (((1,), (1,)), ((), ())), preferred_element_type=F32)


def dot_nn(a, b):
    return jnp.dot(a, b, preferred_element_type=F32)


def score_pair(qt_ref, k_ref, bias_ref, s_ref, mask, pair):
    here = pl.ds(pair * 128, 128)
    first = lax.broadcasted_iota(jnp.int32, (TOK, 128), 1) < TOK
    zero = jnp.zeros((32, 128), BF)
    for group in range(3):
        keys = k_ref[here, pl.ds(group * 128, 128)]
        for half in range(2):
            base = group * 4 + 2 * half
            columns = []
            for j in range(2):
                blocks = [zero] * 4
                blocks[2 * half + j] = qt_ref[pl.ds((base + j) * 32, 32), here]
                columns.append(jnp.concatenate(blocks, axis=0))
            scores = dot_nn(keys, jnp.concatenate(columns, axis=1))
            for j in range(2):
                both = scores[:, j * 128 : (j + 1) * 128]
                s_ref[pair % 2, base + j] = jnp.where(first, both[:TOK], both[TOK:]) + (bias_ref[base + j] + mask)


def weigh_pair(s_ref, p_ref, pair):
    side = lax.broadcasted_iota(jnp.int32, (1, 128), 1) < TOK
    for head in range(HEADS):
        s = s_ref[pair % 2, head]
        e = jnp.exp2(s - jnp.max(s, axis=0, keepdims=True))
        inv = 1.0 / jnp.sum(e, axis=0, keepdims=True)
        lanes = pl.ds(head % 2 * 128, 128)
        p_ref[pair % 2, head // 2, :TOK, lanes] = (e * jnp.where(side, inv, 0.0)).astype(BF)
        p_ref[pair % 2, head // 2, TOK:, lanes] = (e * jnp.where(side, 0.0, inv)).astype(BF)


def mix_pair(vt_ref, p_ref, ot_ref, pair):
    here = pl.ds(pair * 128, 128)
    for two in range(HEADS // 2):
        mixed = dot_nn(vt_ref[pl.ds(two * 64, 64), here], p_ref[pair % 2, two])
        ot_ref[pl.ds(two * 64, 32), here] = mixed[:32, :128]
        ot_ref[pl.ds(two * 64 + 32, 32), here] = mixed[32:, 128:]


def attend_stages(qt_ref, k_ref, vt_ref, bias_ref, s_ref, p_ref, ot_ref, ocean, pairs):
    key = lax.broadcasted_iota(jnp.int32, (TOK, 128), 0)
    lane = lax.broadcasted_iota(jnp.int32, (TOK, 128), 1)

    def score(pair):
        flags = jnp.where(lane < TOK, ocean(2 * pair), ocean(2 * pair + 1))
        mask = jnp.where((lane % TOK == key) | (flags > 0.5), 0.0, -BIG)
        score_pair(qt_ref, k_ref, bias_ref, s_ref, mask, pair)

    stages = [lambda: score(0)]
    for pair in range(pairs):
        if pair + 1 < pairs:
            stages.append(lambda pair=pair: score(pair + 1))
        stages.append(lambda pair=pair: weigh_pair(s_ref, p_ref, pair))
        stages.append(lambda pair=pair: mix_pair(vt_ref, p_ref, ot_ref, pair))
    return stages


def finish_stages(x_tile, mixed_ref, mid_ref, n_ref, hid_ref, proj_ref, gain, up_ref, down_ref, store):
    def head():
        for tile in range(8):
            for r in range(WIN):
                mid_ref[pl.ds(tile * TOK + r * WIN, WIN), :] = x_tile(r, tile).astype(F32)
        mid = (mid_ref[...] + dot_nn(mixed_ref[...], proj_ref[...])).astype(BF).astype(F32)
        mid_ref[...] = mid
        n_ref[...] = normed(mid, gain)

    def up(at):
        lanes = pl.ds(at, UP_CHUNK)
        hid_ref[:, lanes] = jax.nn.gelu(dot_nn(n_ref[...], up_ref[:, lanes]), approximate=True).astype(BF)

    def down():
        result = mid_ref[...] + dot_nn(hid_ref[...], down_ref[...])
        for tile in range(8):
            for r in range(WIN):
                store(r, tile, result[tile * TOK + r * WIN : tile * TOK + (r + 1) * WIN].astype(BF))

    return [head] + [functools.partial(up, at) for at in range(0, HID, UP_CHUNK)] + [down]


def run(order, first, second):
    first, second = list(first), list(second)
    for which in order:
        stages = first if which == "a" else second
        if stages:
            stages.pop(0)()
    for stage in first + second:
        stage()


def project(x_win, gain, qkv_ref, wt_ref, qt_ref, k_ref, vt_ref):
    packed = normed(x_win, gain)
    qt_ref[...] = (dot_nt(wt_ref[:C], packed) * QSCALE).astype(BF)
    k_ref[...] = dot_nn(packed, qkv_ref[:, C : 2 * C]).astype(BF)
    vt_ref[...] = dot_nt(wt_ref[C:], packed).astype(BF)


def prepare(qkv_ref, table_ref, select_ref, wt_ref, tab_ref, row_ref, bias_ref):
    wt_ref[:C] = qkv_ref[:, :C].T
    wt_ref[C:] = qkv_ref[:, 2 * C :].T
    tab_ref[...] = jnp.zeros_like(tab_ref)
    tab_ref[:HEADS, : SPAN * SPAN] = table_ref[...] * LOG2E
    high = tab_ref[...].astype(BF)
    low = (tab_ref[...] - high.astype(F32)).astype(BF)
    picked = dot_nn(high, select_ref[...]) + dot_nn(low, select_ref[...])
    for key in range(WIN):
        for head in range(HEADS):
            row_ref[head, key : key + 1] = picked[head : head + 1, key * 128 : (key + 1) * 128]
    first = lax.broadcasted_iota(jnp.int32, (WIN, 128), 1) < TOK
    for head in range(HEADS):
        rows = row_ref[head]
        for row in range(WIN):
            back = (WIN - 1 - row) * WIN
            left = pltpu.roll(rows, (128 - back) % 128, 1)
            right = pltpu.roll(rows, (TOK - back) % 128, 1)
            bias_ref[head, row * WIN : (row + 1) * WIN] = jnp.where(first, left, right)


def first_kernel(x_ref, before_ref, land_ref, gain_ref, qkv_ref, table_ref, select_ref, proj_ref, up_ref, down_ref, spread_ref, pick_ref,
                 out_ref, wt_ref, tab_ref, row_ref, bias_ref, xw_ref, qt_ref, k_ref, vt_ref, s_ref, p_ref, ot_ref,
                 mixed_ref, mid_ref, n_ref, hid_ref, ocean_ref, flag_ref):
    windows = 8
    step = pl.program_id(0)
    last = pl.num_programs(0) - 1

    def enter():
        flags = (1 - land_ref[...]).astype(F32)
        rows = jnp.broadcast_to(flags[:, None, :], (WIN, WIN, windows * WIN)).reshape(TOK, windows * WIN)
        ocean_ref[...] = dot_nn((rows * spread_ref[...]).astype(BF), pick_ref[...])
        for r in range(WIN):
            for w in range(windows):
                xw_ref[pl.ds(w * TOK + r * WIN, WIN), :] = x_ref[0, r, pl.ds(w * WIN, WIN), :].astype(F32)

    def pack():
        project(xw_ref[...], gain_ref[0:1], qkv_ref, wt_ref, qt_ref, k_ref, vt_ref)

    def store(r, tile, value):
        out_ref[r, pl.ds(tile * WIN, WIN), :C] = value
        out_ref[r, pl.ds(tile * WIN, WIN), C:] = flag_ref[pl.ds(r * WIN, WIN), pl.ds(tile * 128, 128)].astype(BF)

    def turn():
        mixed_ref[...] = ot_ref[...].astype(BF).T

    def leave():
        flag_ref[...] = ocean_ref[...]

    attend = attend_stages(qt_ref, k_ref, vt_ref, bias_ref, s_ref, p_ref, ot_ref, lambda w: ocean_ref[:, pl.ds(w * 128, 128)], windows // 2)
    first = [enter, pack, *attend, turn]
    second = finish_stages(lambda r, t: before_ref[0, r, pl.ds(t * WIN, WIN), :], mixed_ref, mid_ref, n_ref, hid_ref,
                           proj_ref, gain_ref[1:2], up_ref, down_ref, store)

    @pl.when(step == 0)
    def _():
        prepare(qkv_ref, table_ref, select_ref, wt_ref, tab_ref, row_ref, bias_ref)
        run("", first, [])
        leave()

    @pl.when((step > 0) & (step < last))
    def _():
        run(ORDER_FIRST, first, second)
        leave()

    @pl.when(step == last)
    def _():
        run("", [], second)


def second_kernel(low_ref, high_ref, low_side_ref, high_side_ref, above_ref, below_ref, own_ref,
                  gain_ref, qkv_ref, table_ref, select_ref, proj_ref, up_ref, down_ref,
                  out_ref, wt_ref, tab_ref, row_ref, bias_ref, xw_ref, qt_ref, k_ref, vt_ref, s_ref, p_ref, ot_ref,
                  mixed_ref, mid_ref, n_ref, hid_ref, o_ref, carry_ref):
    windows = 9
    step = pl.program_id(0)
    last = pl.num_programs(0) - 1
    low_wide = lax.broadcasted_iota(jnp.int32, (WIN, WIDE), 0) < SHIFT
    low = lax.broadcasted_iota(jnp.int32, (TOK, C), 0) % WIN < SHIFT

    def enter():
        for r in range(WIN):
            near, side, far, edge = (low_ref, low_side_ref, above_ref, step == 0) if r < SHIFT else (high_ref, high_side_ref, below_ref, step == last - 1)
            tiles = []
            for t in range(windows):
                inner = near[r % SHIFT, pl.ds(t * WIN, WIN), :] if t < 8 else side[r % SHIFT]
                tiles.append(jnp.where(edge, far[r % SHIFT, pl.ds(t * WIN, WIN), :].astype(F32), inner.astype(F32)))
            for w in range(windows):
                xw_ref[pl.ds(w * TOK + r * WIN, WIN), :] = jnp.where(low_wide, tiles[w], tiles[(w - 1) % windows])

    def pack():
        project(xw_ref[:, :C], gain_ref[2:3], qkv_ref, wt_ref, qt_ref, k_ref, vt_ref)

    def store(r, tile, value):
        out_ref[0, r, pl.ds(tile * WIN, WIN), :] = value

    def turn():
        o_ref[...] = ot_ref[...].T
        for t in range(8):
            rows = jnp.where(low, o_ref[pl.ds(t * TOK, TOK), :], o_ref[pl.ds((t + 1) * TOK, TOK), :]).astype(BF)
            mixed_ref[pl.ds(t * TOK, TOK // 2), :] = carry_ref[pl.ds(t * TOK // 2, TOK // 2), :]
            mixed_ref[pl.ds(t * TOK + TOK // 2, TOK // 2), :] = rows[: TOK // 2]
            carry_ref[pl.ds(t * TOK // 2, TOK // 2), :] = rows[TOK // 2 :]

    attend = attend_stages(qt_ref, k_ref, vt_ref, bias_ref, s_ref, p_ref, ot_ref, lambda w: xw_ref[pl.ds(w * TOK, TOK), C:], 5)
    first = [enter, pack, *attend, turn]
    second = finish_stages(lambda r, t: own_ref[r, pl.ds(t * WIN, WIN), :], mixed_ref, mid_ref, n_ref, hid_ref,
                           proj_ref, gain_ref[3:4], up_ref, down_ref, store)

    @pl.when(step == 0)
    def _():
        prepare(qkv_ref, table_ref, select_ref, wt_ref, tab_ref, row_ref, bias_ref)
        xw_ref[pl.ds(windows * TOK, TOK), :] = jnp.zeros((TOK, WIDE), F32)
        carry_ref[...] = jnp.zeros_like(carry_ref)

    @pl.when(step < 2)
    def _():
        run("", first, [])

    @pl.when((step >= 2) & (step < last))
    def _():
        run(ORDER_SECOND, first, second)

    @pl.when(step == last)
    def _():
        run("", [], second)


def whole(*shape):
    return pl.BlockSpec(shape, lambda i: (0,) * len(shape), pipeline_mode=pl.Buffered(1))


def of_layer(layer, *shape):
    return pl.BlockSpec((None, *shape), lambda i: (layer, 0, 0), pipeline_mode=pl.Buffered(1))


def weight_specs(layer):
    return [
        whole(4, C),
        of_layer(layer, C, 3 * C),
        of_layer(layer, HEADS, SPAN * SPAN),
        whole(256, WIN * 128),
        of_layer(layer, C, C),
        of_layer(layer, C, HID),
        of_layer(layer, HID, C),
    ]


def scratch(tokens, width):
    return [
        pltpu.VMEM((2 * C, C), BF),
        pltpu.VMEM((16, 256), F32),
        pltpu.VMEM((HEADS, WIN, 128), F32),
        pltpu.VMEM((HEADS, TOK, 128), F32),
        pltpu.VMEM((tokens, width), F32),
        pltpu.VMEM((C, tokens), BF),
        pltpu.VMEM((tokens, C), BF),
        pltpu.VMEM((C, tokens), BF),
        pltpu.VMEM((2, HEADS, TOK, 128), F32),
        pltpu.VMEM((2, HEADS // 2, 128, 256), BF),
        pltpu.VMEM((C, tokens), F32),
        pltpu.VMEM((8 * TOK, C), BF),
        pltpu.VMEM((8 * TOK, C), F32),
        pltpu.VMEM((8 * TOK, C), BF),
        pltpu.VMEM((8 * TOK, HID), BF),
    ]


PARAMS = pltpu.CompilerParams(vmem_limit_bytes=56 << 20)


def first_layer(fields, land, weights):
    _, rows, cols, _ = fields.shape
    windows = cols // WIN
    tokens = windows * TOK
    bands = rows // WIN
    spread, pick = flag_matrices(windows)
    return pl.pallas_call(
        first_kernel,
        grid=(bands + 1,),
        in_specs=[
            pl.BlockSpec((1, WIN, cols, C), lambda i: (0, jnp.minimum(i, bands - 1), 0, 0)),
            pl.BlockSpec((1, WIN, cols, C), lambda i: (0, jnp.maximum(i - 1, 0), 0, 0)),
            pl.BlockSpec((WIN, cols), lambda i: (jnp.minimum(i, bands - 1), 0)),
            *weight_specs(0),
            whole(*spread.shape),
            whole(*pick.shape),
        ],
        out_specs=pl.BlockSpec((WIN, cols, WIDE), lambda i: (jnp.maximum(i - 1, 0), 0, 0)),
        out_shape=jax.ShapeDtypeStruct((rows, cols, WIDE), BF),
        scratch_shapes=[*scratch(tokens, C), pltpu.VMEM((TOK, windows * 128), F32), pltpu.VMEM((TOK, windows * 128), F32)],
        compiler_params=PARAMS,
        name="first_layer",
    )(fields, fields, land, *weights(False), jnp.asarray(spread), jnp.asarray(pick, BF))


def second_layer(own, side, above, below, weights):
    rows, cols, _ = own.shape
    bands = rows // WIN
    tokens = (cols // WIN + 2) * TOK
    lower = lambda i: (jnp.clip(2 * i - 1, 0, 2 * bands - 1), 0, 0)
    upper = lambda i: (jnp.minimum(2 * i, 2 * bands - 1), 0, 0)
    done = lambda i: jnp.maximum(i - 2, 0)
    return pl.pallas_call(
        second_kernel,
        grid=(bands + 2,),
        in_specs=[
            pl.BlockSpec((SHIFT, cols, WIDE), lower),
            pl.BlockSpec((SHIFT, cols, WIDE), upper),
            pl.BlockSpec((SHIFT, WIN, WIDE), lower),
            pl.BlockSpec((SHIFT, WIN, WIDE), upper),
            whole(SHIFT, cols + WIN, WIDE),
            whole(SHIFT, cols + WIN, WIDE),
            pl.BlockSpec((WIN, cols, C), lambda i: (done(i), 0, 0)),
            *weight_specs(1),
        ],
        out_specs=pl.BlockSpec((1, WIN, cols, C), lambda i: (0, done(i), 0, 0)),
        out_shape=jax.ShapeDtypeStruct((1, rows, cols, C), BF),
        scratch_shapes=[*scratch(tokens, WIDE), pltpu.VMEM((tokens, C), F32), pltpu.VMEM((bands * TOK // 2, C), BF)],
        compiler_params=PARAMS,
        name="second_layer",
    )(own, own, side, side, above, below, own, *weights(True))


def ring(axis, periodic):
    count = lax.axis_size(axis)
    forward = [(i, i + 1) for i in range(count - 1)]
    if periodic:
        forward.append((count - 1, 0))
    return forward, [(b, a) for a, b in forward]


def borders(block):
    forward, backward = ring("lon", True)
    left = lax.ppermute(block[:, -SHIFT:], "lon", forward)
    right = lax.ppermute(block[:, :SHIFT], "lon", backward)
    side = jnp.concatenate([right, left], axis=1)
    forward, backward = ring("lat", False)
    above = lax.ppermute(jnp.concatenate([block[-SHIFT:], side[-SHIFT:]], axis=1), "lat", forward)
    below = lax.ppermute(jnp.concatenate([block[:SHIFT], side[:SHIFT]], axis=1), "lat", backward)
    return side, above, below


def shards(fields, land, norm_gains, qkv_weight, rel_bias, proj_weight, up_weight, down_weight):
    def weights(shifted):
        return (norm_gains, qkv_weight, rel_bias, jnp.asarray(bias_selector(shifted), BF), proj_weight, up_weight, down_weight)

    settled = first_layer(fields, land, weights)
    return second_layer(settled, *borders(settled), weights)


def solution(mesh):
    return jax.shard_map(
        shards,
        mesh=mesh,
        in_specs=(P(None, "lat", "lon", None), P("lat", "lon"), P(), P(), P(), P(), P(), P()),
        out_specs=P(None, "lat", "lon", None),
        check_vma=False,
    )
```

```python
import functools

import jax
import jax.numpy as jnp
import numpy as np
from jax import lax
from jax.experimental import pallas as pl
from jax.experimental.pallas import tpu as pltpu
from jax.sharding import PartitionSpec as P

HEADS = 12
WIN = 8
SHIFT = 4
EPS = 1e-05
C = 384
HID = 1536
TOK = WIN * WIN
BIG = 1e30
LOG2E = 1.4426950408889634
QSCALE = LOG2E / (C // HEADS) ** 0.5
BF = jnp.bfloat16
UP_CHUNK = 256
FINE = True
LAG = 2
DOWN_PARTS = 2
AHEAD = 0.0
COSTS = (22, 22, 18)
F32 = jnp.float32


WIDE = C + 128
SPAN = 2 * WIN - 1


def bias_selector(shifted):
    slot = np.arange(WIN)
    col = (slot + SHIFT) % WIN if shifted else slot
    table = np.zeros((256, WIN, 128), np.float32)
    for key in range(WIN):
        for far in range(SPAN):
            for query in range(WIN):
                table[far * SPAN + col[query] - col[key] + WIN - 1, key, far * WIN + query] = 1.0
    return table.reshape(256, WIN * 128)


def flag_matrices(windows):
    slot = np.arange(TOK) % WIN
    lane = np.arange(windows * WIN)
    spread = lane[None, :] % WIN == slot[:, None]
    pick = lane[:, None] // WIN == np.repeat(np.arange(windows), 128)[None, :]
    return spread.astype(np.float32), pick.astype(np.float32)


def normed(values, gain):
    center = jnp.mean(values, axis=-1, keepdims=True)
    moved = values - center
    spread = jnp.mean(moved * moved, axis=-1, keepdims=True)
    return (moved * lax.rsqrt(spread + EPS) * gain).astype(BF)


def dot_nt(a, b):
    return lax.dot_general(a, b, (((1,), (1,)), ((), ())), preferred_element_type=F32)


def dot_nn(a, b):
    return jnp.dot(a, b, preferred_element_type=F32)


def score_two(qt_ref, k_ref, bias_ref, s_ref, mask_ref, pair, two):
    here = pl.ds(pair * 128, 128)
    first = lax.broadcasted_iota(jnp.int32, (TOK, 128), 1) < TOK
    zero = jnp.zeros((32, 128), BF)
    keys = k_ref[here, pl.ds(two // 2 * 128, 128)]
    columns = []
    for j in range(2):
        blocks = [zero] * 4
        blocks[two % 2 * 2 + j] = qt_ref[pl.ds((2 * two + j) * 32, 32), here]
        columns.append(jnp.concatenate(blocks, axis=0))
    scores = dot_nn(keys, jnp.concatenate(columns, axis=1))
    for j in range(2):
        both = scores[:, j * 128 : (j + 1) * 128]
        s_ref[pair % 2, 2 * two + j] = jnp.where(first, both[:TOK], both[TOK:]) + (bias_ref[2 * two + j] + mask_ref[pair % 2])


def weigh_head(s_ref, p_ref, pair, head):
    side = lax.broadcasted_iota(jnp.int32, (1, 128), 1) < TOK
    s = s_ref[pair % 2, head]
    e = jnp.exp2(s - jnp.max(s, axis=0, keepdims=True))
    inv = 1.0 / jnp.sum(e, axis=0, keepdims=True)
    lanes = pl.ds(head % 2 * 128, 128)
    p_ref[pair % 2, head // 2, :TOK, lanes] = (e * jnp.where(side, inv, 0.0)).astype(BF)
    p_ref[pair % 2, head // 2, TOK:, lanes] = (e * jnp.where(side, 0.0, inv)).astype(BF)


def mix_two(vt_ref, p_ref, ot_ref, pair, two):
    here = pl.ds(pair * 128, 128)
    mixed = dot_nn(vt_ref[pl.ds(two * 64, 64), here], p_ref[pair % 2, two])
    ot_ref[pl.ds(two * 64, 32), here] = mixed[:32, :128]
    ot_ref[pl.ds(two * 64 + 32, 32), here] = mixed[32:, 128:]


def attend_stages(qt_ref, k_ref, vt_ref, bias_ref, s_ref, p_ref, ot_ref, mask_ref, ocean, pairs):
    key = lax.broadcasted_iota(jnp.int32, (TOK, 128), 0)
    lane = lax.broadcasted_iota(jnp.int32, (TOK, 128), 1)
    half = HEADS // 2

    def mask(pair):
        flags = jnp.where(lane < TOK, ocean(2 * pair), ocean(2 * pair + 1))
        mask_ref[pair % 2] = jnp.where((lane % TOK == key) | (flags > 0.5), 0.0, -BIG)

    def score(pair, two):
        if two == 0:
            mask(pair)
        score_two(qt_ref, k_ref, bias_ref, s_ref, mask_ref, pair, two)

    def weigh(pair, two):
        weigh_head(s_ref, p_ref, pair, 2 * two)
        weigh_head(s_ref, p_ref, pair, 2 * two + 1)

    stages = [(COSTS[0], functools.partial(score, 0, two)) for two in range(half)]
    for pair in range(pairs):
        if FINE:
            for two in range(half):
                if pair + 1 < pairs:
                    stages.append((COSTS[0], functools.partial(score, pair + 1, two)))
                stages.append((COSTS[1], functools.partial(weigh, pair, two)))
                if two >= LAG:
                    stages.append((COSTS[2], functools.partial(mix_two, vt_ref, p_ref, ot_ref, pair, two - LAG)))
            for two in range(half - LAG, half):
                stages.append((COSTS[2], functools.partial(mix_two, vt_ref, p_ref, ot_ref, pair, two)))
        else:
            if pair + 1 < pairs:
                stages += [(COSTS[0], functools.partial(score, pair + 1, two)) for two in range(half)]
            stages += [(COSTS[1], functools.partial(weigh, pair, two)) for two in range(half)]
            stages += [(COSTS[2], functools.partial(mix_two, vt_ref, p_ref, ot_ref, pair, two)) for two in range(half)]
    return stages


def finish_stages(x_tile, mixed_ref, mid_ref, n_ref, hid_ref, proj_ref, gain, up_ref, down_ref, store):
    def head():
        for tile in range(8):
            for r in range(WIN):
                mid_ref[pl.ds(tile * TOK + r * WIN, WIN), :] = x_tile(r, tile).astype(F32)
        mid_ref[...] = (mid_ref[...] + dot_nn(mixed_ref[...], proj_ref[...])).astype(BF).astype(F32)

    def norm(at):
        rows = pl.ds(at, 128)
        n_ref[rows, :] = normed(mid_ref[rows, :], gain)

    def up(at):
        lanes = pl.ds(at, UP_CHUNK)
        hid_ref[:, lanes] = jax.nn.gelu(dot_nn(n_ref[...], up_ref[:, lanes]), approximate=True).astype(BF)

    def down(part):
        rows = 8 * TOK // DOWN_PARTS
        here = pl.ds(part * rows, rows)
        result = mid_ref[here, :] + dot_nn(hid_ref[here, :], down_ref[...])
        for tile in range(8 // DOWN_PARTS):
            for r in range(WIN):
                store(r, part * 8 // DOWN_PARTS + tile, result[tile * TOK + r * WIN : tile * TOK + (r + 1) * WIN])

    return (
        [(300, head)]
        + [(40, functools.partial(norm, at)) for at in range(0, 8 * TOK, 128)]
        + [(0.7 * UP_CHUNK, functools.partial(up, at)) for at in range(0, HID, UP_CHUNK)]
        + [(800 // DOWN_PARTS, functools.partial(down, part)) for part in range(DOWN_PARTS)]
    )


def run(first, second, shift=0.0):
    ends = []
    for which, stages, ahead in ((0, first, 0.0), (1, second, shift)):
        total = sum(cost for cost, _ in stages) or 1
        done = 0
        for cost, stage in stages:
            done += cost
            ends.append(((done - cost * 0.5) / total - ahead, which, len(ends), stage))
    for _, _, _, stage in sorted(ends, key=lambda e: e[:3]):
        stage()


def project_stages(x_ref, packed_ref, gain, qkv_ref, wt_ref, qt_ref, k_ref, vt_ref):
    def norm(at):
        rows = pl.ds(at, 128)
        packed_ref[rows, :] = normed(x_ref[rows, :C], gain)

    def queries():
        qt_ref[...] = (dot_nt(wt_ref[:C], packed_ref[...]) * QSCALE).astype(BF)

    def keys():
        k_ref[...] = dot_nn(packed_ref[...], qkv_ref[:, C : 2 * C]).astype(BF)

    def values():
        vt_ref[...] = dot_nt(wt_ref[C:], packed_ref[...]).astype(BF)

    tokens = packed_ref.shape[0]
    return [(40, functools.partial(norm, at)) for at in range(0, tokens, 128)] + [(250, keys), (250, queries), (250, values)]


def prepare(layer, qkv_ref, table_ref, select_ref, wt_ref, tab_ref, row_ref, bias_ref):
    wt_ref[:C] = qkv_ref[:, :C].T
    wt_ref[C:] = qkv_ref[:, 2 * C :].T
    tab_ref[...] = jnp.zeros_like(tab_ref)
    tab_ref[:HEADS, : SPAN * SPAN] = table_ref[:, layer] * LOG2E
    high = tab_ref[...].astype(BF)
    low = (tab_ref[...] - high.astype(F32)).astype(BF)
    picked = dot_nn(high, select_ref[...]) + dot_nn(low, select_ref[...])
    for key in range(WIN):
        for head in range(HEADS):
            row_ref[head, key : key + 1] = picked[head : head + 1, key * 128 : (key + 1) * 128]
    first = lax.broadcasted_iota(jnp.int32, (WIN, 128), 1) < TOK
    for head in range(HEADS):
        rows = row_ref[head]
        for row in range(WIN):
            back = (WIN - 1 - row) * WIN
            left = pltpu.roll(rows, (128 - back) % 128, 1)
            right = pltpu.roll(rows, (TOK - back) % 128, 1)
            bias_ref[head, row * WIN : (row + 1) * WIN] = jnp.where(first, left, right)


def first_kernel(x_ref, before_ref, land_ref, gain_ref, qkv_ref, table_ref, select_ref, proj_ref, up_ref, down_ref, spread_ref, pick_ref,
                 out_ref, begin_ref, end_ref, wt_ref, tab_ref, row_ref, bias_ref, xw_ref, qt_ref, k_ref, vt_ref, s_ref, p_ref, ot_ref,
                 packed_ref, mask_ref, mixed_ref, mid_ref, n_ref, hid_ref, ocean_ref, flag_ref):
    windows = 8
    step = pl.program_id(0)
    last = pl.num_programs(0) - 1

    def enter():
        flags = (1 - land_ref[...]).astype(F32)
        rows = jnp.broadcast_to(flags[:, None, :], (WIN, WIN, windows * WIN)).reshape(TOK, windows * WIN)
        ocean_ref[...] = dot_nn((rows * spread_ref[...]).astype(BF), pick_ref[...])
        for r in range(WIN):
            for w in range(windows):
                xw_ref[pl.ds(w * TOK + r * WIN, WIN), :] = x_ref[0, r, pl.ds(w * WIN, WIN), :].astype(F32)

    def store(r, tile, value):
        flag = flag_ref[pl.ds(r * WIN, WIN), pl.ds(tile * 128, 128)]
        out_ref[r, pl.ds(tile * WIN, WIN), :C] = value.astype(BF)
        out_ref[r, pl.ds(tile * WIN, WIN), C:] = flag.astype(BF)
        if tile == 0:
            begin_ref[r, :, :C] = value[:SHIFT].astype(BF)
            begin_ref[r, :, C:] = flag[:SHIFT].astype(BF)
        if tile == windows - 1:
            end_ref[r, :, :C] = value[SHIFT:].astype(BF)
            end_ref[r, :, C:] = flag[SHIFT:].astype(BF)

    def turn():
        mixed_ref[...] = ot_ref[...].astype(BF).T

    def leave():
        flag_ref[...] = ocean_ref[...]

    attend = attend_stages(qt_ref, k_ref, vt_ref, bias_ref, s_ref, p_ref, ot_ref, mask_ref, lambda w: ocean_ref[:, pl.ds(w * 128, 128)], windows // 2)
    pack = project_stages(xw_ref, packed_ref, gain_ref[0:1], qkv_ref, wt_ref, qt_ref, k_ref, vt_ref)
    first = [(200, enter), *pack, *attend, (150, turn)]
    second = finish_stages(lambda r, t: before_ref[0, r, pl.ds(t * WIN, WIN), :], mixed_ref, mid_ref, n_ref, hid_ref,
                           proj_ref, gain_ref[1:2], up_ref, down_ref, store)

    @pl.when(step == 0)
    def _():
        prepare(0, qkv_ref, table_ref, select_ref, wt_ref, tab_ref, row_ref, bias_ref)
        run(first, [])
        leave()

    @pl.when((step > 0) & (step < last))
    def _():
        run(first, second, AHEAD)
        leave()

    @pl.when(step == last)
    def _():
        run([], second)


def second_kernel(low_ref, high_ref, low_right_ref, high_right_ref, low_left_ref, high_left_ref, above_ref, below_ref, own_ref,
                  gain_ref, qkv_ref, table_ref, select_ref, proj_ref, up_ref, down_ref,
                  out_ref, wt_ref, tab_ref, row_ref, bias_ref, xw_ref, qt_ref, k_ref, vt_ref, s_ref, p_ref, ot_ref, packed_ref, mask_ref,
                  mixed_ref, mid_ref, n_ref, hid_ref, o_ref, carry_ref):
    windows = 9
    step = pl.program_id(0)
    last = pl.num_programs(0) - 1
    low_wide = lax.broadcasted_iota(jnp.int32, (WIN, WIDE), 0) < SHIFT
    low = lax.broadcasted_iota(jnp.int32, (TOK, C), 0) % WIN < SHIFT

    def enter():
        for r in range(WIN):
            near, right, left, far, edge = (
                (low_ref, low_right_ref, low_left_ref, above_ref, step == 0)
                if r < SHIFT
                else (high_ref, high_right_ref, high_left_ref, below_ref, step == last - 1)
            )
            tiles = []
            for t in range(windows):
                if t < 8:
                    inner = near[r % SHIFT, pl.ds(t * WIN, WIN), :].astype(F32)
                else:
                    inner = jnp.concatenate([right[r % SHIFT].astype(F32), left[r % SHIFT].astype(F32)], axis=0)
                tiles.append(jnp.where(edge, far[r % SHIFT, pl.ds(t * WIN, WIN), :].astype(F32), inner))
            for w in range(windows):
                xw_ref[pl.ds(w * TOK + r * WIN, WIN), :] = jnp.where(low_wide, tiles[w], tiles[(w - 1) % windows])

    def store(r, tile, value):
        out_ref[0, r, pl.ds(tile * WIN, WIN), :] = value.astype(BF)

    def turn():
        o_ref[...] = ot_ref[...].T
        for t in range(8):
            rows = jnp.where(low, o_ref[pl.ds(t * TOK, TOK), :], o_ref[pl.ds((t + 1) * TOK, TOK), :]).astype(BF)
            mixed_ref[pl.ds(t * TOK, TOK // 2), :] = carry_ref[pl.ds(t * TOK // 2, TOK // 2), :]
            mixed_ref[pl.ds(t * TOK + TOK // 2, TOK // 2), :] = rows[: TOK // 2]
            carry_ref[pl.ds(t * TOK // 2, TOK // 2), :] = rows[TOK // 2 :]

    attend = attend_stages(qt_ref, k_ref, vt_ref, bias_ref, s_ref, p_ref, ot_ref, mask_ref, lambda w: xw_ref[pl.ds(w * TOK, TOK), C:], 5)
    pack = project_stages(xw_ref, packed_ref, gain_ref[2:3], qkv_ref, wt_ref, qt_ref, k_ref, vt_ref)
    first = [(250, enter), *pack, *attend, (200, turn)]
    second = finish_stages(lambda r, t: own_ref[r, pl.ds(t * WIN, WIN), :], mixed_ref, mid_ref, n_ref, hid_ref,
                           proj_ref, gain_ref[3:4], up_ref, down_ref, store)

    @pl.when(step == 0)
    def _():
        prepare(1, qkv_ref, table_ref, select_ref, wt_ref, tab_ref, row_ref, bias_ref)
        xw_ref[pl.ds(windows * TOK, TOK), :] = jnp.zeros((TOK, WIDE), F32)
        carry_ref[...] = jnp.zeros_like(carry_ref)

    @pl.when(step < 2)
    def _():
        run(first, [])

    @pl.when((step >= 2) & (step < last))
    def _():
        run(first, second, AHEAD)

    @pl.when(step == last)
    def _():
        run([], second)


def whole(*shape):
    return pl.BlockSpec(shape, lambda i: (0,) * len(shape), pipeline_mode=pl.Buffered(1))


def of_layer(layer, *shape):
    return pl.BlockSpec((None, *shape), lambda i: (layer, 0, 0), pipeline_mode=pl.Buffered(1))


def weight_specs(layer):
    return [
        whole(4, C),
        of_layer(layer, C, 3 * C),
        whole(HEADS, 2, SPAN * SPAN),
        whole(256, WIN * 128),
        of_layer(layer, C, C),
        of_layer(layer, C, HID),
        of_layer(layer, HID, C),
    ]


def scratch(tokens, width):
    return [
        pltpu.VMEM((2 * C, C), BF),
        pltpu.VMEM((16, 256), F32),
        pltpu.VMEM((HEADS, WIN, 128), F32),
        pltpu.VMEM((HEADS, TOK, 128), F32),
        pltpu.VMEM((tokens, width), F32),
        pltpu.VMEM((C, tokens), BF),
        pltpu.VMEM((tokens, C), BF),
        pltpu.VMEM((C, tokens), BF),
        pltpu.VMEM((2, HEADS, TOK, 128), F32),
        pltpu.VMEM((2, HEADS // 2, 128, 256), BF),
        pltpu.VMEM((C, tokens), F32),
        pltpu.VMEM((tokens, C), BF),
        pltpu.VMEM((2, TOK, 128), F32),
        pltpu.VMEM((8 * TOK, C), BF),
        pltpu.VMEM((8 * TOK, C), F32),
        pltpu.VMEM((8 * TOK, C), BF),
        pltpu.VMEM((8 * TOK, HID), BF),
    ]


PARAMS = pltpu.CompilerParams(vmem_limit_bytes=56 << 20)


def first_layer(fields, land, weights):
    _, rows, cols, _ = fields.shape
    windows = cols // WIN
    tokens = windows * TOK
    bands = rows // WIN
    spread, pick = flag_matrices(windows)
    return pl.pallas_call(
        first_kernel,
        grid=(bands + 1,),
        in_specs=[
            pl.BlockSpec((1, WIN, cols, C), lambda i: (0, jnp.minimum(i, bands - 1), 0, 0)),
            pl.BlockSpec((1, WIN, cols, C), lambda i: (0, jnp.maximum(i - 1, 0), 0, 0)),
            pl.BlockSpec((WIN, cols), lambda i: (jnp.minimum(i, bands - 1), 0)),
            *weight_specs(0),
            whole(*spread.shape),
            whole(*pick.shape),
        ],
        out_specs=[pl.BlockSpec((WIN, width, WIDE), lambda i: (jnp.maximum(i - 1, 0), 0, 0)) for width in (cols, SHIFT, SHIFT)],
        out_shape=[jax.ShapeDtypeStruct((rows, width, WIDE), BF) for width in (cols, SHIFT, SHIFT)],
        scratch_shapes=[*scratch(tokens, C), pltpu.VMEM((TOK, windows * 128), F32), pltpu.VMEM((TOK, windows * 128), F32)],
        compiler_params=PARAMS,
        name="first_layer",
    )(fields, fields, land, *weights(False), jnp.asarray(spread), jnp.asarray(pick, BF))


def second_layer(own, right, left, above, below, weights):
    rows, cols, _ = own.shape
    bands = rows // WIN
    tokens = (cols // WIN + 2) * TOK
    lower = lambda i: (jnp.clip(2 * i - 1, 0, 2 * bands - 1), 0, 0)
    upper = lambda i: (jnp.minimum(2 * i, 2 * bands - 1), 0, 0)
    done = lambda i: jnp.maximum(i - 2, 0)
    return pl.pallas_call(
        second_kernel,
        grid=(bands + 2,),
        in_specs=[
            pl.BlockSpec((SHIFT, cols, WIDE), lower),
            pl.BlockSpec((SHIFT, cols, WIDE), upper),
            pl.BlockSpec((SHIFT, SHIFT, WIDE), lower),
            pl.BlockSpec((SHIFT, SHIFT, WIDE), upper),
            pl.BlockSpec((SHIFT, SHIFT, WIDE), lower),
            pl.BlockSpec((SHIFT, SHIFT, WIDE), upper),
            pl.BlockSpec(memory_space=pltpu.VMEM),
            pl.BlockSpec(memory_space=pltpu.VMEM),
            pl.BlockSpec((WIN, cols, C), lambda i: (done(i), 0, 0)),
            *weight_specs(1),
        ],
        out_specs=pl.BlockSpec((1, WIN, cols, C), lambda i: (0, done(i), 0, 0)),
        out_shape=jax.ShapeDtypeStruct((1, rows, cols, C), BF),
        scratch_shapes=[*scratch(tokens, WIDE), pltpu.VMEM((tokens, C), F32), pltpu.VMEM((bands * TOK // 2, C), BF)],
        compiler_params=PARAMS,
        name="second_layer",
    )(own, own, right, right, left, left, above, below, own, *weights(True))


def ring(axis, periodic):
    count = lax.axis_size(axis)
    forward = [(i, i + 1) for i in range(count - 1)]
    if periodic:
        forward.append((count - 1, 0))
    return forward, [(b, a) for a, b in forward]


def borders(block, begin, end):
    forward, backward = ring("lon", True)
    left = lax.ppermute(end, "lon", forward)
    right = lax.ppermute(begin, "lon", backward)
    forward, backward = ring("lat", False)
    above = lax.ppermute(jnp.concatenate([part[-SHIFT:] for part in (block, right, left)], axis=1), "lat", forward)
    below = lax.ppermute(jnp.concatenate([part[:SHIFT] for part in (block, right, left)], axis=1), "lat", backward)
    return right, left, above, below


def shards(fields, land, norm_gains, qkv_weight, rel_bias, proj_weight, up_weight, down_weight):
    def weights(shifted):
        return (norm_gains, qkv_weight, rel_bias.transpose(1, 0, 2), jnp.asarray(bias_selector(shifted), BF), proj_weight, up_weight, down_weight)

    settled, begin, end = first_layer(fields, land, weights)
    return second_layer(settled, *borders(settled, begin, end), weights)


def solution(mesh):
    return jax.shard_map(
        shards,
        mesh=mesh,
        in_specs=(P(None, "lat", "lon", None), P("lat", "lon"), P(), P(), P(), P(), P(), P()),
        out_specs=P(None, "lat", "lon", None),
        check_vma=False,
    )
```

```python
import functools

import jax
import jax.numpy as jnp
import numpy as np
from jax import lax
from jax.experimental import pallas as pl
from jax.experimental.pallas import tpu as pltpu
from jax.sharding import PartitionSpec as P

HEADS = 12
WIN = 8
SHIFT = 4
EPS = 1e-05
C = 384
HID = 1536
TOK = WIN * WIN
BIG = 1e30
LOG2E = 1.4426950408889634
QSCALE = LOG2E / (C // HEADS) ** 0.5
BF = jnp.bfloat16
GELU_SCALE = (2.0 / np.pi) ** 0.5
UP_CHUNK = 256
FINE = True
LAG = 2
DOWN_PARTS = 2
AHEAD = 0.0
COSTS = (22, 22, 18)
F32 = jnp.float32
GELU = BF


WIDE = C + 128
SPAN = 2 * WIN - 1


def bias_selector(shifted):
    slot = np.arange(WIN)
    col = (slot + SHIFT) % WIN if shifted else slot
    table = np.zeros((256, WIN, 128), np.float32)
    for key in range(WIN):
        for far in range(SPAN):
            for query in range(WIN):
                table[far * SPAN + col[query] - col[key] + WIN - 1, key, far * WIN + query] = 1.0
    return table.reshape(256, WIN * 128)


def flag_matrices(windows):
    slot = np.arange(TOK) % WIN
    lane = np.arange(windows * WIN)
    spread = lane[None, :] % WIN == slot[:, None]
    pick = lane[:, None] // WIN == np.repeat(np.arange(windows), 128)[None, :]
    return spread.astype(np.float32), pick.astype(np.float32)


def normed(values, gain):
    center = jnp.mean(values, axis=-1, keepdims=True)
    moved = values - center
    spread = jnp.mean(moved * moved, axis=-1, keepdims=True)
    return (moved * lax.rsqrt(spread + EPS) * gain).astype(BF)


def gelu(x):
    x = x.astype(GELU)
    inner = x * (x * x * GELU(0.044715 * GELU_SCALE) + GELU(GELU_SCALE))
    return (x * GELU(0.5) * (jnp.tanh(inner) + GELU(1.0))).astype(BF)


def dot_nt(a, b):
    return lax.dot_general(a, b, (((1,), (1,)), ((), ())), preferred_element_type=F32)


def dot_nn(a, b):
    return jnp.dot(a, b, preferred_element_type=F32)


def score_two(qt_ref, k_ref, bias_ref, s_ref, mask_ref, pair, two):
    here = pl.ds(pair * 128, 128)
    first = lax.broadcasted_iota(jnp.int32, (TOK, 128), 1) < TOK
    zero = jnp.zeros((32, 128), BF)
    keys = k_ref[here, pl.ds(two // 2 * 128, 128)]
    columns = []
    for j in range(2):
        blocks = [zero] * 4
        blocks[two % 2 * 2 + j] = qt_ref[pl.ds((2 * two + j) * 32, 32), here]
        columns.append(jnp.concatenate(blocks, axis=0))
    scores = dot_nn(keys, jnp.concatenate(columns, axis=1))
    for j in range(2):
        both = scores[:, j * 128 : (j + 1) * 128]
        s_ref[pair % 2, 2 * two + j] = jnp.where(first, both[:TOK], both[TOK:]) + (bias_ref[2 * two + j] + mask_ref[pair % 2])


def weigh_head(s_ref, p_ref, pair, head):
    side = lax.broadcasted_iota(jnp.int32, (1, 128), 1) < TOK
    s = s_ref[pair % 2, head]
    e = jnp.exp2(s - jnp.max(s, axis=0, keepdims=True))
    inv = 1.0 / jnp.sum(e, axis=0, keepdims=True)
    lanes = pl.ds(head % 2 * 128, 128)
    p_ref[pair % 2, head // 2, :TOK, lanes] = (e * jnp.where(side, inv, 0.0)).astype(BF)
    p_ref[pair % 2, head // 2, TOK:, lanes] = (e * jnp.where(side, 0.0, inv)).astype(BF)


def mix_two(vt_ref, p_ref, ot_ref, pair, two):
    here = pl.ds(pair * 128, 128)
    mixed = dot_nn(vt_ref[pl.ds(two * 64, 64), here], p_ref[pair % 2, two])
    ot_ref[pl.ds(two * 64, 32), here] = mixed[:32, :128]
    ot_ref[pl.ds(two * 64 + 32, 32), here] = mixed[32:, 128:]


def attend_stages(qt_ref, k_ref, vt_ref, bias_ref, s_ref, p_ref, ot_ref, mask_ref, ocean, pairs):
    key = lax.broadcasted_iota(jnp.int32, (TOK, 128), 0)
    lane = lax.broadcasted_iota(jnp.int32, (TOK, 128), 1)
    half = HEADS // 2

    def mask(pair):
        flags = jnp.where(lane < TOK, ocean(2 * pair), ocean(2 * pair + 1))
        mask_ref[pair % 2] = jnp.where((lane % TOK == key) | (flags > 0.5), 0.0, -BIG)

    def score(pair, two):
        if two == 0:
            mask(pair)
        score_two(qt_ref, k_ref, bias_ref, s_ref, mask_ref, pair, two)

    def weigh(pair, two):
        weigh_head(s_ref, p_ref, pair, 2 * two)
        weigh_head(s_ref, p_ref, pair, 2 * two + 1)

    stages = [(COSTS[0], functools.partial(score, 0, two)) for two in range(half)]
    for pair in range(pairs):
        if FINE:
            for two in range(half):
                if pair + 1 < pairs:
                    stages.append((COSTS[0], functools.partial(score, pair + 1, two)))
                stages.append((COSTS[1], functools.partial(weigh, pair, two)))
                if two >= LAG:
                    stages.append((COSTS[2], functools.partial(mix_two, vt_ref, p_ref, ot_ref, pair, two - LAG)))
            for two in range(half - LAG, half):
                stages.append((COSTS[2], functools.partial(mix_two, vt_ref, p_ref, ot_ref, pair, two)))
        else:
            if pair + 1 < pairs:
                stages += [(COSTS[0], functools.partial(score, pair + 1, two)) for two in range(half)]
            stages += [(COSTS[1], functools.partial(weigh, pair, two)) for two in range(half)]
            stages += [(COSTS[2], functools.partial(mix_two, vt_ref, p_ref, ot_ref, pair, two)) for two in range(half)]
    return stages


def finish_stages(x_tile, mixed_ref, mid_ref, n_ref, hid_ref, proj_ref, gain, up_ref, down_ref, store):
    def head():
        for tile in range(8):
            for r in range(WIN):
                mid_ref[pl.ds(tile * TOK + r * WIN, WIN), :] = x_tile(r, tile).astype(F32)
        mid_ref[...] = (mid_ref[...] + dot_nn(mixed_ref[...], proj_ref[...])).astype(BF).astype(F32)

    def norm(at):
        rows = pl.ds(at, 128)
        n_ref[rows, :] = normed(mid_ref[rows, :], gain)

    def up(at):
        lanes = pl.ds(at, UP_CHUNK)
        hid_ref[:, lanes] = gelu(dot_nn(n_ref[...], up_ref[:, lanes]))

    def down(part):
        rows = 8 * TOK // DOWN_PARTS
        here = pl.ds(part * rows, rows)
        result = mid_ref[here, :] + dot_nn(hid_ref[here, :], down_ref[...])
        for tile in range(8 // DOWN_PARTS):
            for r in range(WIN):
                store(r, part * 8 // DOWN_PARTS + tile, result[tile * TOK + r * WIN : tile * TOK + (r + 1) * WIN])

    return (
        [(300, head)]
        + [(40, functools.partial(norm, at)) for at in range(0, 8 * TOK, 128)]
        + [(0.7 * UP_CHUNK, functools.partial(up, at)) for at in range(0, HID, UP_CHUNK)]
        + [(800 // DOWN_PARTS, functools.partial(down, part)) for part in range(DOWN_PARTS)]
    )


def run(first, second, shift=0.0):
    ends = []
    for which, stages, ahead in ((0, first, 0.0), (1, second, shift)):
        total = sum(cost for cost, _ in stages) or 1
        done = 0
        for cost, stage in stages:
            done += cost
            ends.append(((done - cost * 0.5) / total - ahead, which, len(ends), stage))
    for _, _, _, stage in sorted(ends, key=lambda e: e[:3]):
        stage()


def project_stages(x_ref, packed_ref, gain, qkv_ref, wt_ref, qt_ref, k_ref, vt_ref):
    def norm(at):
        rows = pl.ds(at, 128)
        packed_ref[rows, :] = normed(x_ref[rows, :C], gain)

    def queries():
        qt_ref[...] = (dot_nt(wt_ref[:C], packed_ref[...]) * QSCALE).astype(BF)

    def keys():
        k_ref[...] = dot_nn(packed_ref[...], qkv_ref[:, C : 2 * C]).astype(BF)

    def values():
        vt_ref[...] = dot_nt(wt_ref[C:], packed_ref[...]).astype(BF)

    tokens = packed_ref.shape[0]
    return [(40, functools.partial(norm, at)) for at in range(0, tokens, 128)] + [(250, keys), (250, queries), (250, values)]


def prepare(layer, qkv_ref, table_ref, select_ref, wt_ref, tab_ref, row_ref, bias_ref):
    wt_ref[:C] = qkv_ref[:, :C].T
    wt_ref[C:] = qkv_ref[:, 2 * C :].T
    tab_ref[...] = jnp.zeros_like(tab_ref)
    tab_ref[:HEADS, : SPAN * SPAN] = table_ref[:, layer] * LOG2E
    high = tab_ref[...].astype(BF)
    low = (tab_ref[...] - high.astype(F32)).astype(BF)
    picked = dot_nn(high, select_ref[...]) + dot_nn(low, select_ref[...])
    for key in range(WIN):
        for head in range(HEADS):
            row_ref[head, key : key + 1] = picked[head : head + 1, key * 128 : (key + 1) * 128]
    first = lax.broadcasted_iota(jnp.int32, (WIN, 128), 1) < TOK
    for head in range(HEADS):
        rows = row_ref[head]
        for row in range(WIN):
            back = (WIN - 1 - row) * WIN
            left = pltpu.roll(rows, (128 - back) % 128, 1)
            right = pltpu.roll(rows, (TOK - back) % 128, 1)
            bias_ref[head, row * WIN : (row + 1) * WIN] = jnp.where(first, left, right)


def first_kernel(x_ref, before_ref, land_ref, gain_ref, qkv_ref, table_ref, select_ref, proj_ref, up_ref, down_ref, spread_ref, pick_ref,
                 out_ref, begin_ref, end_ref, wt_ref, tab_ref, row_ref, bias_ref, xw_ref, qt_ref, k_ref, vt_ref, s_ref, p_ref, ot_ref,
                 packed_ref, mask_ref, mixed_ref, mid_ref, n_ref, hid_ref, ocean_ref, flag_ref):
    windows = 8
    step = pl.program_id(0)
    last = pl.num_programs(0) - 1

    def enter():
        flags = (1 - land_ref[...]).astype(F32)
        rows = jnp.broadcast_to(flags[:, None, :], (WIN, WIN, windows * WIN)).reshape(TOK, windows * WIN)
        ocean_ref[...] = dot_nn((rows * spread_ref[...]).astype(BF), pick_ref[...])
        for r in range(WIN):
            for w in range(windows):
                xw_ref[pl.ds(w * TOK + r * WIN, WIN), :] = x_ref[0, r, pl.ds(w * WIN, WIN), :].astype(F32)

    def store(r, tile, value):
        flag = flag_ref[pl.ds(r * WIN, WIN), pl.ds(tile * 128, 128)]
        out_ref[r, pl.ds(tile * WIN, WIN), :C] = value.astype(BF)
        out_ref[r, pl.ds(tile * WIN, WIN), C:] = flag.astype(BF)
        if tile == 0:
            begin_ref[r, :, :C] = value[:SHIFT].astype(BF)
            begin_ref[r, :, C:] = flag[:SHIFT].astype(BF)
        if tile == windows - 1:
            end_ref[r, :, :C] = value[SHIFT:].astype(BF)
            end_ref[r, :, C:] = flag[SHIFT:].astype(BF)

    def turn():
        mixed_ref[...] = ot_ref[...].astype(BF).T

    def leave():
        flag_ref[...] = ocean_ref[...]

    attend = attend_stages(qt_ref, k_ref, vt_ref, bias_ref, s_ref, p_ref, ot_ref, mask_ref, lambda w: ocean_ref[:, pl.ds(w * 128, 128)], windows // 2)
    pack = project_stages(xw_ref, packed_ref, gain_ref[0:1], qkv_ref, wt_ref, qt_ref, k_ref, vt_ref)
    first = [(200, enter), *pack, *attend, (150, turn)]
    second = finish_stages(lambda r, t: before_ref[0, r, pl.ds(t * WIN, WIN), :], mixed_ref, mid_ref, n_ref, hid_ref,
                           proj_ref, gain_ref[1:2], up_ref, down_ref, store)

    @pl.when(step == 0)
    def _():
        prepare(0, qkv_ref, table_ref, select_ref, wt_ref, tab_ref, row_ref, bias_ref)
        run(first, [])
        leave()

    @pl.when((step > 0) & (step < last))
    def _():
        run(first, second, AHEAD)
        leave()

    @pl.when(step == last)
    def _():
        run([], second)


def second_kernel(low_ref, high_ref, low_right_ref, high_right_ref, low_left_ref, high_left_ref, above_ref, below_ref, own_ref,
                  gain_ref, qkv_ref, table_ref, select_ref, proj_ref, up_ref, down_ref,
                  out_ref, wt_ref, tab_ref, row_ref, bias_ref, xw_ref, qt_ref, k_ref, vt_ref, s_ref, p_ref, ot_ref, packed_ref, mask_ref,
                  mixed_ref, mid_ref, n_ref, hid_ref, o_ref, carry_ref):
    windows = 9
    step = pl.program_id(0)
    last = pl.num_programs(0) - 1
    low_wide = lax.broadcasted_iota(jnp.int32, (WIN, WIDE), 0) < SHIFT
    low = lax.broadcasted_iota(jnp.int32, (TOK, C), 0) % WIN < SHIFT

    def enter():
        for r in range(WIN):
            near, right, left, far, edge = (
                (low_ref, low_right_ref, low_left_ref, above_ref, step == 0)
                if r < SHIFT
                else (high_ref, high_right_ref, high_left_ref, below_ref, step == last - 1)
            )
            tiles = []
            for t in range(windows):
                if t < 8:
                    inner = near[r % SHIFT, pl.ds(t * WIN, WIN), :].astype(F32)
                else:
                    inner = jnp.concatenate([right[r % SHIFT].astype(F32), left[r % SHIFT].astype(F32)], axis=0)
                tiles.append(jnp.where(edge, far[r % SHIFT, pl.ds(t * WIN, WIN), :].astype(F32), inner))
            for w in range(windows):
                xw_ref[pl.ds(w * TOK + r * WIN, WIN), :] = jnp.where(low_wide, tiles[w], tiles[(w - 1) % windows])

    def store(r, tile, value):
        out_ref[0, r, pl.ds(tile * WIN, WIN), :] = value.astype(BF)

    def turn():
        o_ref[...] = ot_ref[...].T
        for t in range(8):
            rows = jnp.where(low, o_ref[pl.ds(t * TOK, TOK), :], o_ref[pl.ds((t + 1) * TOK, TOK), :]).astype(BF)
            mixed_ref[pl.ds(t * TOK, TOK // 2), :] = carry_ref[pl.ds(t * TOK // 2, TOK // 2), :]
            mixed_ref[pl.ds(t * TOK + TOK // 2, TOK // 2), :] = rows[: TOK // 2]
            carry_ref[pl.ds(t * TOK // 2, TOK // 2), :] = rows[TOK // 2 :]

    attend = attend_stages(qt_ref, k_ref, vt_ref, bias_ref, s_ref, p_ref, ot_ref, mask_ref, lambda w: xw_ref[pl.ds(w * TOK, TOK), C:], 5)
    pack = project_stages(xw_ref, packed_ref, gain_ref[2:3], qkv_ref, wt_ref, qt_ref, k_ref, vt_ref)
    first = [(250, enter), *pack, *attend, (200, turn)]
    second = finish_stages(lambda r, t: own_ref[r, pl.ds(t * WIN, WIN), :], mixed_ref, mid_ref, n_ref, hid_ref,
                           proj_ref, gain_ref[3:4], up_ref, down_ref, store)

    @pl.when(step == 0)
    def _():
        prepare(1, qkv_ref, table_ref, select_ref, wt_ref, tab_ref, row_ref, bias_ref)
        xw_ref[pl.ds(windows * TOK, TOK), :] = jnp.zeros((TOK, WIDE), F32)
        carry_ref[...] = jnp.zeros_like(carry_ref)

    @pl.when(step < 2)
    def _():
        run(first, [])

    @pl.when((step >= 2) & (step < last))
    def _():
        run(first, second, AHEAD)

    @pl.when(step == last)
    def _():
        run([], second)


def whole(*shape):
    return pl.BlockSpec(shape, lambda i: (0,) * len(shape), pipeline_mode=pl.Buffered(1))


def of_layer(layer, *shape):
    return pl.BlockSpec((None, *shape), lambda i: (layer, 0, 0), pipeline_mode=pl.Buffered(1))


def weight_specs(layer):
    return [
        whole(4, C),
        of_layer(layer, C, 3 * C),
        whole(HEADS, 2, SPAN * SPAN),
        whole(256, WIN * 128),
        of_layer(layer, C, C),
        of_layer(layer, C, HID),
        of_layer(layer, HID, C),
    ]


def scratch(tokens, width):
    return [
        pltpu.VMEM((2 * C, C), BF),
        pltpu.VMEM((16, 256), F32),
        pltpu.VMEM((HEADS, WIN, 128), F32),
        pltpu.VMEM((HEADS, TOK, 128), F32),
        pltpu.VMEM((tokens, width), F32),
        pltpu.VMEM((C, tokens), BF),
        pltpu.VMEM((tokens, C), BF),
        pltpu.VMEM((C, tokens), BF),
        pltpu.VMEM((2, HEADS, TOK, 128), F32),
        pltpu.VMEM((2, HEADS // 2, 128, 256), BF),
        pltpu.VMEM((C, tokens), F32),
        pltpu.VMEM((tokens, C), BF),
        pltpu.VMEM((2, TOK, 128), F32),
        pltpu.VMEM((8 * TOK, C), BF),
        pltpu.VMEM((8 * TOK, C), F32),
        pltpu.VMEM((8 * TOK, C), BF),
        pltpu.VMEM((8 * TOK, HID), BF),
    ]


PARAMS = pltpu.CompilerParams(vmem_limit_bytes=56 << 20)


def first_layer(fields, land, weights):
    _, rows, cols, _ = fields.shape
    windows = cols // WIN
    tokens = windows * TOK
    bands = rows // WIN
    spread, pick = flag_matrices(windows)
    return pl.pallas_call(
        first_kernel,
        grid=(bands + 1,),
        in_specs=[
            pl.BlockSpec((1, WIN, cols, C), lambda i: (0, jnp.minimum(i, bands - 1), 0, 0)),
            pl.BlockSpec((1, WIN, cols, C), lambda i: (0, jnp.maximum(i - 1, 0), 0, 0)),
            pl.BlockSpec((WIN, cols), lambda i: (jnp.minimum(i, bands - 1), 0)),
            *weight_specs(0),
            whole(*spread.shape),
            whole(*pick.shape),
        ],
        out_specs=[pl.BlockSpec((WIN, width, WIDE), lambda i: (jnp.maximum(i - 1, 0), 0, 0)) for width in (cols, SHIFT, SHIFT)],
        out_shape=[jax.ShapeDtypeStruct((rows, width, WIDE), BF) for width in (cols, SHIFT, SHIFT)],
        scratch_shapes=[*scratch(tokens, C), pltpu.VMEM((TOK, windows * 128), F32), pltpu.VMEM((TOK, windows * 128), F32)],
        compiler_params=PARAMS,
        name="first_layer",
    )(fields, fields, land, *weights(False), jnp.asarray(spread), jnp.asarray(pick, BF))


def second_layer(own, right, left, above, below, weights):
    rows, cols, _ = own.shape
    bands = rows // WIN
    tokens = (cols // WIN + 2) * TOK
    lower = lambda i: (jnp.clip(2 * i - 1, 0, 2 * bands - 1), 0, 0)
    upper = lambda i: (jnp.minimum(2 * i, 2 * bands - 1), 0, 0)
    done = lambda i: jnp.maximum(i - 2, 0)
    return pl.pallas_call(
        second_kernel,
        grid=(bands + 2,),
        in_specs=[
            pl.BlockSpec((SHIFT, cols, WIDE), lower),
            pl.BlockSpec((SHIFT, cols, WIDE), upper),
            pl.BlockSpec((SHIFT, SHIFT, WIDE), lower),
            pl.BlockSpec((SHIFT, SHIFT, WIDE), upper),
            pl.BlockSpec((SHIFT, SHIFT, WIDE), lower),
            pl.BlockSpec((SHIFT, SHIFT, WIDE), upper),
            pl.BlockSpec(memory_space=pltpu.VMEM),
            pl.BlockSpec(memory_space=pltpu.VMEM),
            pl.BlockSpec((WIN, cols, C), lambda i: (done(i), 0, 0)),
            *weight_specs(1),
        ],
        out_specs=pl.BlockSpec((1, WIN, cols, C), lambda i: (0, done(i), 0, 0)),
        out_shape=jax.ShapeDtypeStruct((1, rows, cols, C), BF),
        scratch_shapes=[*scratch(tokens, WIDE), pltpu.VMEM((tokens, C), F32), pltpu.VMEM((bands * TOK // 2, C), BF)],
        compiler_params=PARAMS,
        name="second_layer",
    )(own, own, right, right, left, left, above, below, own, *weights(True))


def ring(axis, periodic):
    count = lax.axis_size(axis)
    forward = [(i, i + 1) for i in range(count - 1)]
    if periodic:
        forward.append((count - 1, 0))
    return forward, [(b, a) for a, b in forward]


def borders(block, begin, end):
    forward, backward = ring("lon", True)
    left = lax.ppermute(end, "lon", forward)
    right = lax.ppermute(begin, "lon", backward)
    forward, backward = ring("lat", False)
    above = lax.ppermute(jnp.concatenate([part[-SHIFT:] for part in (block, right, left)], axis=1), "lat", forward)
    below = lax.ppermute(jnp.concatenate([part[:SHIFT] for part in (block, right, left)], axis=1), "lat", backward)
    return right, left, above, below


def shards(fields, land, norm_gains, qkv_weight, rel_bias, proj_weight, up_weight, down_weight):
    def weights(shifted):
        return (norm_gains, qkv_weight, rel_bias.transpose(1, 0, 2), jnp.asarray(bias_selector(shifted), BF), proj_weight, up_weight, down_weight)

    settled, begin, end = first_layer(fields, land, weights)
    return second_layer(settled, *borders(settled, begin, end), weights)


def solution(mesh):
    return jax.shard_map(
        shards,
        mesh=mesh,
        in_specs=(P(None, "lat", "lon", None), P("lat", "lon"), P(), P(), P(), P(), P(), P()),
        out_specs=P(None, "lat", "lon", None),
        check_vma=False,
    )
```

```python
import functools

import jax
import jax.numpy as jnp
import numpy as np
from jax import lax
from jax.experimental import pallas as pl
from jax.experimental.pallas import tpu as pltpu
from jax.sharding import PartitionSpec as P

HEADS = 12
WIN = 8
SHIFT = 4
EPS = 1e-05
C = 384
HID = 1536
TOK = WIN * WIN
BIG = 1e30
LOG2E = 1.4426950408889634
QSCALE = LOG2E / (C // HEADS) ** 0.5
BF = jnp.bfloat16
GELU_SCALE = (2.0 / np.pi) ** 0.5
UP_CHUNK = 256
FINE = True
LAG = 2
DOWN_PARTS = 2
AHEAD = 0.0
COSTS = (22, 22, 18)
F32 = jnp.float32
GELU = BF


WIDE = C + 128
SPAN = 2 * WIN - 1


def bias_selector(shifted):
    slot = np.arange(WIN)
    col = (slot + SHIFT) % WIN if shifted else slot
    table = np.zeros((256, WIN, 128), np.float32)
    for key in range(WIN):
        for far in range(SPAN):
            for query in range(WIN):
                table[far * SPAN + col[query] - col[key] + WIN - 1, key, far * WIN + query] = 1.0
    return table.reshape(256, WIN * 128)


def flag_matrices(windows):
    slot = np.arange(TOK) % WIN
    lane = np.arange(windows * WIN)
    spread = lane[None, :] % WIN == slot[:, None]
    pick = lane[:, None] // WIN == np.repeat(np.arange(windows), 128)[None, :]
    return spread.astype(np.float32), pick.astype(np.float32)


def normed(values, gain):
    center = jnp.mean(values, axis=-1, keepdims=True)
    moved = values - center
    spread = jnp.mean(moved * moved, axis=-1, keepdims=True)
    return (moved * lax.rsqrt(spread + EPS) * gain).astype(BF)


def gelu(x):
    x = x.astype(GELU)
    inner = x * (x * x * GELU(0.044715 * GELU_SCALE) + GELU(GELU_SCALE))
    return (x * GELU(0.5) * (jnp.tanh(inner) + GELU(1.0))).astype(BF)


def dot_nt(a, b):
    return lax.dot_general(a, b, (((1,), (1,)), ((), ())), preferred_element_type=F32)


def dot_nn(a, b):
    return jnp.dot(a, b, preferred_element_type=F32)


def score_two(qt_ref, k_ref, bias_ref, s_ref, mask_ref, pair, two):
    here = pl.ds(pair * 128, 128)
    first = lax.broadcasted_iota(jnp.int32, (TOK, 128), 1) < TOK
    zero = jnp.zeros((32, 128), BF)
    keys = k_ref[here, pl.ds(two // 2 * 128, 128)]
    columns = []
    for j in range(2):
        blocks = [zero] * 4
        blocks[two % 2 * 2 + j] = qt_ref[pl.ds((2 * two + j) * 32, 32), here]
        columns.append(jnp.concatenate(blocks, axis=0))
    scores = dot_nn(keys, jnp.concatenate(columns, axis=1))
    for j in range(2):
        both = scores[:, j * 128 : (j + 1) * 128]
        s_ref[pair % 2, 2 * two + j] = jnp.where(first, both[:TOK], both[TOK:]) + (bias_ref[2 * two + j] + mask_ref[pair % 2])


def weigh_head(s_ref, p_ref, pair, head):
    side = (lax.broadcasted_iota(jnp.int32, (TOK, 128), 1) < TOK).astype(F32)
    s = s_ref[pair % 2, head]
    e = jnp.exp2(s - jnp.max(s, axis=0, keepdims=True)).astype(BF)
    lanes = pl.ds(head % 2 * 128, 128)
    p_ref[pair % 2, head // 2, :TOK, lanes] = e * side.astype(BF)
    p_ref[pair % 2, head // 2, TOK:, lanes] = e * (1.0 - side).astype(BF)


def mix_two(vt_ref, p_ref, ot_ref, pair, two):
    here = pl.ds(pair * 128, 128)
    rows = jnp.concatenate([vt_ref[pl.ds(two * 64, 64), here], jnp.ones((16, 128), BF)], axis=0)
    mixed = dot_nn(rows, p_ref[pair % 2, two])
    inv = 1.0 / mixed[64:72]
    inv = jnp.concatenate([inv] * 4, axis=0)
    ot_ref[pl.ds(two * 64, 32), here] = mixed[:32, :128] * inv[:, :128]
    ot_ref[pl.ds(two * 64 + 32, 32), here] = mixed[32:64, 128:] * inv[:, 128:]


def attend_stages(qt_ref, k_ref, vt_ref, bias_ref, s_ref, p_ref, ot_ref, mask_ref, ocean, pairs):
    key = lax.broadcasted_iota(jnp.int32, (TOK, 128), 0)
    lane = lax.broadcasted_iota(jnp.int32, (TOK, 128), 1)
    half = HEADS // 2

    def mask(pair):
        flags = jnp.where(lane < TOK, ocean(2 * pair), ocean(2 * pair + 1))
        mask_ref[pair % 2] = jnp.where((lane % TOK == key) | (flags > 0.5), 0.0, -BIG)

    def score(pair, two):
        if two == 0:
            mask(pair)
        score_two(qt_ref, k_ref, bias_ref, s_ref, mask_ref, pair, two)

    def weigh(pair, two):
        weigh_head(s_ref, p_ref, pair, 2 * two)
        weigh_head(s_ref, p_ref, pair, 2 * two + 1)

    stages = [(COSTS[0], functools.partial(score, 0, two)) for two in range(half)]
    for pair in range(pairs):
        if FINE:
            for two in range(half):
                if pair + 1 < pairs:
                    stages.append((COSTS[0], functools.partial(score, pair + 1, two)))
                stages.append((COSTS[1], functools.partial(weigh, pair, two)))
                if two >= LAG:
                    stages.append((COSTS[2], functools.partial(mix_two, vt_ref, p_ref, ot_ref, pair, two - LAG)))
            for two in range(half - LAG, half):
                stages.append((COSTS[2], functools.partial(mix_two, vt_ref, p_ref, ot_ref, pair, two)))
        else:
            if pair + 1 < pairs:
                stages += [(COSTS[0], functools.partial(score, pair + 1, two)) for two in range(half)]
            stages += [(COSTS[1], functools.partial(weigh, pair, two)) for two in range(half)]
            stages += [(COSTS[2], functools.partial(mix_two, vt_ref, p_ref, ot_ref, pair, two)) for two in range(half)]
    return stages


def finish_stages(x_tile, mixed_ref, mid_ref, n_ref, hid_ref, proj_ref, gain, up_ref, down_ref, store):
    def head():
        for tile in range(8):
            for r in range(WIN):
                mid_ref[pl.ds(tile * TOK + r * WIN, WIN), :] = x_tile(r, tile).astype(F32)
        mid_ref[...] = (mid_ref[...] + dot_nn(mixed_ref[...], proj_ref[...])).astype(BF).astype(F32)

    def norm(at):
        rows = pl.ds(at, 128)
        n_ref[rows, :] = normed(mid_ref[rows, :], gain)

    def up(at):
        lanes = pl.ds(at, UP_CHUNK)
        hid_ref[:, lanes] = gelu(dot_nn(n_ref[...], up_ref[:, lanes]))

    def down(part):
        rows = 8 * TOK // DOWN_PARTS
        here = pl.ds(part * rows, rows)
        result = mid_ref[here, :] + dot_nn(hid_ref[here, :], down_ref[...])
        for tile in range(8 // DOWN_PARTS):
            for r in range(WIN):
                store(r, part * 8 // DOWN_PARTS + tile, result[tile * TOK + r * WIN : tile * TOK + (r + 1) * WIN])

    return (
        [(300, head)]
        + [(40, functools.partial(norm, at)) for at in range(0, 8 * TOK, 128)]
        + [(0.7 * UP_CHUNK, functools.partial(up, at)) for at in range(0, HID, UP_CHUNK)]
        + [(800 // DOWN_PARTS, functools.partial(down, part)) for part in range(DOWN_PARTS)]
    )


def run(first, second, shift=0.0):
    ends = []
    for which, stages, ahead in ((0, first, 0.0), (1, second, shift)):
        total = sum(cost for cost, _ in stages) or 1
        done = 0
        for cost, stage in stages:
            done += cost
            ends.append(((done - cost * 0.5) / total - ahead, which, len(ends), stage))
    for _, _, _, stage in sorted(ends, key=lambda e: e[:3]):
        stage()


def project_stages(x_ref, packed_ref, gain, qkv_ref, wt_ref, qt_ref, k_ref, vt_ref):
    def norm(at):
        rows = pl.ds(at, 128)
        packed_ref[rows, :] = normed(x_ref[rows, :C], gain)

    def queries():
        qt_ref[...] = (dot_nt(wt_ref[:C], packed_ref[...]) * QSCALE).astype(BF)

    def keys():
        k_ref[...] = dot_nn(packed_ref[...], qkv_ref[:, C : 2 * C]).astype(BF)

    def values():
        vt_ref[...] = dot_nt(wt_ref[C:], packed_ref[...]).astype(BF)

    tokens = packed_ref.shape[0]
    return [(40, functools.partial(norm, at)) for at in range(0, tokens, 128)] + [(250, keys), (250, queries), (250, values)]


def prepare(layer, qkv_ref, table_ref, select_ref, wt_ref, tab_ref, row_ref, bias_ref):
    wt_ref[:C] = qkv_ref[:, :C].T
    wt_ref[C:] = qkv_ref[:, 2 * C :].T
    tab_ref[...] = jnp.zeros_like(tab_ref)
    tab_ref[:HEADS, : SPAN * SPAN] = table_ref[:, layer] * LOG2E
    high = tab_ref[...].astype(BF)
    low = (tab_ref[...] - high.astype(F32)).astype(BF)
    picked = dot_nn(high, select_ref[...]) + dot_nn(low, select_ref[...])
    for key in range(WIN):
        for head in range(HEADS):
            row_ref[head, key : key + 1] = picked[head : head + 1, key * 128 : (key + 1) * 128]
    first = lax.broadcasted_iota(jnp.int32, (WIN, 128), 1) < TOK
    for head in range(HEADS):
        rows = row_ref[head]
        for row in range(WIN):
            back = (WIN - 1 - row) * WIN
            left = pltpu.roll(rows, (128 - back) % 128, 1)
            right = pltpu.roll(rows, (TOK - back) % 128, 1)
            bias_ref[head, row * WIN : (row + 1) * WIN] = jnp.where(first, left, right)


def first_kernel(x_ref, before_ref, land_ref, gain_ref, qkv_ref, table_ref, select_ref, proj_ref, up_ref, down_ref, spread_ref, pick_ref,
                 out_ref, begin_ref, end_ref, wt_ref, tab_ref, row_ref, bias_ref, xw_ref, qt_ref, k_ref, vt_ref, s_ref, p_ref, ot_ref,
                 packed_ref, mask_ref, mixed_ref, mid_ref, n_ref, hid_ref, ocean_ref, flag_ref):
    windows = 8
    step = pl.program_id(0)
    last = pl.num_programs(0) - 1

    def enter():
        flags = (1 - land_ref[...]).astype(F32)
        rows = jnp.broadcast_to(flags[:, None, :], (WIN, WIN, windows * WIN)).reshape(TOK, windows * WIN)
        ocean_ref[...] = dot_nn((rows * spread_ref[...]).astype(BF), pick_ref[...])
        for r in range(WIN):
            for w in range(windows):
                xw_ref[pl.ds(w * TOK + r * WIN, WIN), :] = x_ref[0, r, pl.ds(w * WIN, WIN), :].astype(F32)

    def store(r, tile, value):
        flag = flag_ref[pl.ds(r * WIN, WIN), pl.ds(tile * 128, 128)]
        out_ref[r, pl.ds(tile * WIN, WIN), :C] = value.astype(BF)
        out_ref[r, pl.ds(tile * WIN, WIN), C:] = flag.astype(BF)
        if tile == 0:
            begin_ref[r, :, :C] = value[:SHIFT].astype(BF)
            begin_ref[r, :, C:] = flag[:SHIFT].astype(BF)
        if tile == windows - 1:
            end_ref[r, :, :C] = value[SHIFT:].astype(BF)
            end_ref[r, :, C:] = flag[SHIFT:].astype(BF)

    def turn():
        mixed_ref[...] = ot_ref[...].astype(BF).T

    def leave():
        flag_ref[...] = ocean_ref[...]

    attend = attend_stages(qt_ref, k_ref, vt_ref, bias_ref, s_ref, p_ref, ot_ref, mask_ref, lambda w: ocean_ref[:, pl.ds(w * 128, 128)], windows // 2)
    pack = project_stages(xw_ref, packed_ref, gain_ref[0:1], qkv_ref, wt_ref, qt_ref, k_ref, vt_ref)
    first = [(200, enter), *pack, *attend, (150, turn)]
    second = finish_stages(lambda r, t: before_ref[0, r, pl.ds(t * WIN, WIN), :], mixed_ref, mid_ref, n_ref, hid_ref,
                           proj_ref, gain_ref[1:2], up_ref, down_ref, store)

    @pl.when(step == 0)
    def _():
        prepare(0, qkv_ref, table_ref, select_ref, wt_ref, tab_ref, row_ref, bias_ref)
        run(first, [])
        leave()

    @pl.when((step > 0) & (step < last))
    def _():
        run(first, second, AHEAD)
        leave()

    @pl.when(step == last)
    def _():
        run([], second)


def second_kernel(low_ref, high_ref, low_right_ref, high_right_ref, low_left_ref, high_left_ref, above_ref, below_ref, own_ref,
                  gain_ref, qkv_ref, table_ref, select_ref, proj_ref, up_ref, down_ref,
                  out_ref, wt_ref, tab_ref, row_ref, bias_ref, xw_ref, qt_ref, k_ref, vt_ref, s_ref, p_ref, ot_ref, packed_ref, mask_ref,
                  mixed_ref, mid_ref, n_ref, hid_ref, o_ref, carry_ref):
    windows = 9
    step = pl.program_id(0)
    last = pl.num_programs(0) - 1
    low_wide = lax.broadcasted_iota(jnp.int32, (WIN, WIDE), 0) < SHIFT
    low = lax.broadcasted_iota(jnp.int32, (TOK, C), 0) % WIN < SHIFT

    def enter():
        for r in range(WIN):
            near, right, left, far, edge = (
                (low_ref, low_right_ref, low_left_ref, above_ref, step == 0)
                if r < SHIFT
                else (high_ref, high_right_ref, high_left_ref, below_ref, step == last - 1)
            )
            tiles = []
            for t in range(windows):
                if t < 8:
                    inner = near[r % SHIFT, pl.ds(t * WIN, WIN), :].astype(F32)
                else:
                    inner = jnp.concatenate([right[r % SHIFT].astype(F32), left[r % SHIFT].astype(F32)], axis=0)
                tiles.append(jnp.where(edge, far[r % SHIFT, pl.ds(t * WIN, WIN), :].astype(F32), inner))
            for w in range(windows):
                xw_ref[pl.ds(w * TOK + r * WIN, WIN), :] = jnp.where(low_wide, tiles[w], tiles[(w - 1) % windows])

    def store(r, tile, value):
        out_ref[0, r, pl.ds(tile * WIN, WIN), :] = value.astype(BF)

    def turn():
        o_ref[...] = ot_ref[...].T
        for t in range(8):
            rows = jnp.where(low, o_ref[pl.ds(t * TOK, TOK), :], o_ref[pl.ds((t + 1) * TOK, TOK), :]).astype(BF)
            mixed_ref[pl.ds(t * TOK, TOK // 2), :] = carry_ref[pl.ds(t * TOK // 2, TOK // 2), :]
            mixed_ref[pl.ds(t * TOK + TOK // 2, TOK // 2), :] = rows[: TOK // 2]
            carry_ref[pl.ds(t * TOK // 2, TOK // 2), :] = rows[TOK // 2 :]

    attend = attend_stages(qt_ref, k_ref, vt_ref, bias_ref, s_ref, p_ref, ot_ref, mask_ref, lambda w: xw_ref[pl.ds(w * TOK, TOK), C:], 5)
    pack = project_stages(xw_ref, packed_ref, gain_ref[2:3], qkv_ref, wt_ref, qt_ref, k_ref, vt_ref)
    first = [(250, enter), *pack, *attend, (200, turn)]
    second = finish_stages(lambda r, t: own_ref[r, pl.ds(t * WIN, WIN), :], mixed_ref, mid_ref, n_ref, hid_ref,
                           proj_ref, gain_ref[3:4], up_ref, down_ref, store)

    @pl.when(step == 0)
    def _():
        prepare(1, qkv_ref, table_ref, select_ref, wt_ref, tab_ref, row_ref, bias_ref)
        xw_ref[pl.ds(windows * TOK, TOK), :] = jnp.zeros((TOK, WIDE), F32)
        carry_ref[...] = jnp.zeros_like(carry_ref)

    @pl.when(step < 2)
    def _():
        run(first, [])

    @pl.when((step >= 2) & (step < last))
    def _():
        run(first, second, AHEAD)

    @pl.when(step == last)
    def _():
        run([], second)


def whole(*shape):
    return pl.BlockSpec(shape, lambda i: (0,) * len(shape), pipeline_mode=pl.Buffered(1))


def of_layer(layer, *shape):
    return pl.BlockSpec((None, *shape), lambda i: (layer, 0, 0), pipeline_mode=pl.Buffered(1))


def weight_specs(layer):
    return [
        whole(4, C),
        of_layer(layer, C, 3 * C),
        whole(HEADS, 2, SPAN * SPAN),
        whole(256, WIN * 128),
        of_layer(layer, C, C),
        of_layer(layer, C, HID),
        of_layer(layer, HID, C),
    ]


def scratch(tokens, width):
    return [
        pltpu.VMEM((2 * C, C), BF),
        pltpu.VMEM((16, 256), F32),
        pltpu.VMEM((HEADS, WIN, 128), F32),
        pltpu.VMEM((HEADS, TOK, 128), F32),
        pltpu.VMEM((tokens, width), F32),
        pltpu.VMEM((C, tokens), BF),
        pltpu.VMEM((tokens, C), BF),
        pltpu.VMEM((C, tokens), BF),
        pltpu.VMEM((2, HEADS, TOK, 128), F32),
        pltpu.VMEM((2, HEADS // 2, 128, 256), BF),
        pltpu.VMEM((C, tokens), F32),
        pltpu.VMEM((tokens, C), BF),
        pltpu.VMEM((2, TOK, 128), F32),
        pltpu.VMEM((8 * TOK, C), BF),
        pltpu.VMEM((8 * TOK, C), F32),
        pltpu.VMEM((8 * TOK, C), BF),
        pltpu.VMEM((8 * TOK, HID), BF),
    ]


PARAMS = pltpu.CompilerParams(vmem_limit_bytes=56 << 20)


def first_layer(fields, land, weights):
    _, rows, cols, _ = fields.shape
    windows = cols // WIN
    tokens = windows * TOK
    bands = rows // WIN
    spread, pick = flag_matrices(windows)
    return pl.pallas_call(
        first_kernel,
        grid=(bands + 1,),
        in_specs=[
            pl.BlockSpec((1, WIN, cols, C), lambda i: (0, jnp.minimum(i, bands - 1), 0, 0)),
            pl.BlockSpec((1, WIN, cols, C), lambda i: (0, jnp.maximum(i - 1, 0), 0, 0)),
            pl.BlockSpec((WIN, cols), lambda i: (jnp.minimum(i, bands - 1), 0)),
            *weight_specs(0),
            whole(*spread.shape),
            whole(*pick.shape),
        ],
        out_specs=[pl.BlockSpec((WIN, width, WIDE), lambda i: (jnp.maximum(i - 1, 0), 0, 0)) for width in (cols, SHIFT, SHIFT)],
        out_shape=[jax.ShapeDtypeStruct((rows, width, WIDE), BF) for width in (cols, SHIFT, SHIFT)],
        scratch_shapes=[*scratch(tokens, C), pltpu.VMEM((TOK, windows * 128), F32), pltpu.VMEM((TOK, windows * 128), F32)],
        compiler_params=PARAMS,
        name="first_layer",
    )(fields, fields, land, *weights(False), jnp.asarray(spread), jnp.asarray(pick, BF))


def second_layer(own, right, left, above, below, weights):
    rows, cols, _ = own.shape
    bands = rows // WIN
    tokens = (cols // WIN + 2) * TOK
    lower = lambda i: (jnp.clip(2 * i - 1, 0, 2 * bands - 1), 0, 0)
    upper = lambda i: (jnp.minimum(2 * i, 2 * bands - 1), 0, 0)
    done = lambda i: jnp.maximum(i - 2, 0)
    return pl.pallas_call(
        second_kernel,
        grid=(bands + 2,),
        in_specs=[
            pl.BlockSpec((SHIFT, cols, WIDE), lower),
            pl.BlockSpec((SHIFT, cols, WIDE), upper),
            pl.BlockSpec((SHIFT, SHIFT, WIDE), lower),
            pl.BlockSpec((SHIFT, SHIFT, WIDE), upper),
            pl.BlockSpec((SHIFT, SHIFT, WIDE), lower),
            pl.BlockSpec((SHIFT, SHIFT, WIDE), upper),
            pl.BlockSpec(memory_space=pltpu.VMEM),
            pl.BlockSpec(memory_space=pltpu.VMEM),
            pl.BlockSpec((WIN, cols, C), lambda i: (done(i), 0, 0)),
            *weight_specs(1),
        ],
        out_specs=pl.BlockSpec((1, WIN, cols, C), lambda i: (0, done(i), 0, 0)),
        out_shape=jax.ShapeDtypeStruct((1, rows, cols, C), BF),
        scratch_shapes=[*scratch(tokens, WIDE), pltpu.VMEM((tokens, C), F32), pltpu.VMEM((bands * TOK // 2, C), BF)],
        compiler_params=PARAMS,
        name="second_layer",
    )(own, own, right, right, left, left, above, below, own, *weights(True))


def ring(axis, periodic):
    count = lax.axis_size(axis)
    forward = [(i, i + 1) for i in range(count - 1)]
    if periodic:
        forward.append((count - 1, 0))
    return forward, [(b, a) for a, b in forward]


def borders(block, begin, end):
    forward, backward = ring("lon", True)
    left = lax.ppermute(end, "lon", forward)
    right = lax.ppermute(begin, "lon", backward)
    forward, backward = ring("lat", False)
    above = lax.ppermute(jnp.concatenate([part[-SHIFT:] for part in (block, right, left)], axis=1), "lat", forward)
    below = lax.ppermute(jnp.concatenate([part[:SHIFT] for part in (block, right, left)], axis=1), "lat", backward)
    return right, left, above, below


def shards(fields, land, norm_gains, qkv_weight, rel_bias, proj_weight, up_weight, down_weight):
    def weights(shifted):
        return (norm_gains, qkv_weight, rel_bias.transpose(1, 0, 2), jnp.asarray(bias_selector(shifted), BF), proj_weight, up_weight, down_weight)

    settled, begin, end = first_layer(fields, land, weights)
    return second_layer(settled, *borders(settled, begin, end), weights)


def solution(mesh):
    return jax.shard_map(
        shards,
        mesh=mesh,
        in_specs=(P(None, "lat", "lon", None), P("lat", "lon"), P(), P(), P(), P(), P(), P()),
        out_specs=P(None, "lat", "lon", None),
        check_vma=False,
    )
```
